32 devices in a mesh: group: 2 (over x), shard: 16 (over z, y, core).
Axes of the slice: x: 2, y: 2, z: 4, core: 2. Of those that a mesh axis runs over, the one named last changes fastest.
Arguments:
- rollout_rows: bfloat16 [512, 8192], P('group', 'shard'), may hold values from -6 to 6
- assign: int32 [512], replicated, may hold values from 0 to 511, each once
- cotangent: bfloat16 [512, 8192], P('group', 'shard'), may hold values from -3 to 3
- w_master: float32 [8192, 8192], P('group', 'shard'), may hold values from -0.0625 to 0.0625
- adam_m: float32 [8192, 8192], P('group', 'shard'), may hold values from -6 to 6
- adam_v: float32 [8192, 8192], P('group', 'shard'), may hold values from 0.05 to 1
- tile_mask: int32 [64, 64], replicated, may hold values from 0 to 1, as said below
Outputs:
- projected: bfloat16 [512, 8192], P('group', 'shard')
- input_grad: bfloat16 [512, 8192], P('group', 'shard')
- w_updated: float32 [8192, 8192], P('group', 'shard')
- m_updated: float32 [8192, 8192], P('group', 'shard')
- v_updated: float32 [8192, 8192], P('group', 'shard')
- rollout_tiles: bfloat16 [64, 6, 128, 128], P('shard')
The draws below stay inside these ranges and needn't reach their ends.
Inputs may be any that keep to these rules, and one draw needn't show every extreme that they name: `tile_mask`: each tile column has 1 to 6 trainable tiles, and some column has exactly 6. `assign`: a permutation of the 512 rollout rows.
All inputs are finite; a program needn't handle non-finite values.
Results may differ from the reference program's by a relative error of at most 0.0051.
Values may be sent and summed in bfloat16 or wider, within the bound.
No kernel may reach another device: no remote copies, remote signals or barrier semaphores. Data moves between devices by JAX's collectives and lax.ppermute only.
A program may use at most 192 MiB of HBM per device.

```python
import math
import jax
import jax.numpy as jnp
from jax import lax

D = 8192
E = 8192
TILE = 128
CAP = 6
TR = 64
TC = 64
N = 512


def draw_tile_mask(key, part):
    key_count = jax.random.fold_in(key, 11)
    key_full = jax.random.fold_in(key, 12)
    key_score = jax.random.fold_in(key, 13)
    counts = jax.random.randint(key_count, (TC,), 1, CAP + 1)
    full_column = jax.random.randint(key_full, (), 0, TC)
    counts = jnp.where(jnp.arange(TC) == full_column, CAP, counts)
    scores = jax.random.randint(key_score, (TR, TC), 0, 2 ** 20) * TR + jnp.arange(TR)[:, None]
    row_order = jnp.argsort(scores, axis=0, stable=True)
    ranks = jnp.argsort(row_order, axis=0, stable=True)
    return (ranks < counts[None, :]).astype(jnp.int32)


def levels(key, extent, shards, low, top_value):
    level, own = 1.0, jax.random.fold_in(key, 6)
    for dim, blocks in shards:
        draws = jnp.exp(jax.random.uniform(jax.random.fold_in(own, dim), (blocks,), jnp.float32, low / len(shards), top_value / len(shards)))
        level = level * jnp.repeat(draws, extent[dim] // blocks).reshape([-1 if axis == dim else 1 for axis in range(len(extent))])
    return level


def gaussian(own_key, extent, scale, limit, shards=(), held_as=jnp.bfloat16):
    values = scale * jax.random.normal(own_key, extent, jnp.float32)
    if shards:
        values = values * levels(own_key, extent, shards, -0.22, 0.18)
    return jnp.clip(values, -limit, limit).astype(held_as)


def setup_inputs(seed: int = 0) -> dict:
    streams_of = jax.random.split(jax.random.key(seed), 8)
    rollout_rows = gaussian(streams_of[0], (N, D), 1.0, 6.0, ((0, 2), (1, 16)))
    assign = jax.random.permutation(streams_of[1], N).astype(jnp.int32)
    cotangent = gaussian(streams_of[2], (N, E), 0.5, 3.0, ((0, 2), (1, 16)))
    w_master = gaussian(streams_of[3], (D, E), D ** -0.5, 0.0625, ((0, 2), (1, 16)), jnp.float32)
    adam_m = gaussian(streams_of[4], (D, E), 1.0, 6.0, ((0, 2), (1, 16)), jnp.float32)
    adam_v = jnp.clip(jnp.exp(math.log(1.0) - 2.9957323 * jax.random.uniform(streams_of[5], (D, E), jnp.float32) ** levels(streams_of[5], (D, E), ((0, 2), (1, 16)), -0.2, 0.2)), 0.05, 1.0)
    tile_mask = draw_tile_mask(jax.random.fold_in(streams_of[7], 71), 0)
    return dict(rollout_rows=rollout_rows, assign=assign, cotangent=cotangent, w_master=w_master, adam_m=adam_m, adam_v=adam_v, tile_mask=tile_mask)


beta_one = 0.9
beta_two = 0.999
learn_rate = 0.02
eps_adam = 1e-08
bias_one = 1.0 - 0.9 ** 10
bias_two = 1.0 - 0.999 ** 10

def slot_rows(tile_mask):
    row_order = jnp.argsort(1 - tile_mask, axis=0, stable=True)
    slot_index = row_order[:CAP].T.astype(jnp.int32)
    counts = lax.optimization_barrier(jnp.sum(tile_mask, axis=0))
    live_slot = jnp.arange(CAP)[None, :] < counts[:, None]
    return (slot_index, live_slot)

def reference(rollout_rows, assign, cotangent, w_master, adam_m, adam_v, tile_mask):
    trained = jnp.take(rollout_rows, assign.astype(jnp.int32), axis=0)
    w_half = w_master.astype(jnp.bfloat16)
    projected = jnp.dot(trained, w_half, preferred_element_type=jnp.float32).astype(jnp.bfloat16)
    input_grad = lax.dot_general(cotangent, w_half, (((1,), (1,)), ((), ())), preferred_element_type=jnp.float32).astype(jnp.bfloat16)
    slot_index, live_slot = slot_rows(tile_mask)
    row_blocks = trained.reshape(N, TR, TILE)

    def one_column(column):
        chosen = row_blocks[:, slot_index[column]].astype(jnp.float32)
        cot_block = lax.dynamic_slice_in_dim(cotangent, column * TILE, TILE, 1).astype(jnp.float32)
        return jnp.einsum('rjk,rl->jkl', chosen, cot_block, precision=lax.Precision.HIGHEST)
    packed = lax.map(one_column, jnp.arange(TC).astype(jnp.int32))
    packed = packed * live_slot[:, :, None, None].astype(jnp.float32)
    columns = jnp.broadcast_to(jnp.arange(TC).astype(jnp.int32)[:, None], (TC, CAP))
    grid = jnp.zeros((TR, TC, TILE, TILE), jnp.float32).at[slot_index, columns].add(packed)
    gradient = grid.transpose(0, 2, 1, 3).reshape(D, E)
    mask_wide = jnp.broadcast_to((tile_mask > 0)[:, None, :, None], (TR, TILE, TC, TILE)).reshape(D, E)
    m_updated = jnp.where(mask_wide, beta_one * adam_m + (1.0 - beta_one) * gradient, adam_m)
    v_updated = jnp.where(mask_wide, beta_two * adam_v + (1.0 - beta_two) * gradient * gradient, adam_v)
    adam_step = m_updated / bias_one / (jnp.sqrt(v_updated / bias_two) + eps_adam)
    w_updated = jnp.where(mask_wide, w_master - learn_rate * adam_step, w_master)
    new_tiles = w_updated.reshape(TR, TILE, TC, TILE).transpose(0, 2, 1, 3)
    picked = new_tiles[slot_index, columns] * live_slot[:, :, None, None].astype(jnp.float32)
    rollout_tiles = picked.astype(jnp.bfloat16)
    return (projected, input_grad, w_updated, m_updated, v_updated, rollout_tiles)
```

```python
import functools

import jax
import jax.numpy as jnp
from jax import lax
from jax.experimental import pallas as pl
from jax.experimental.pallas import tpu as pltpu
from jax.sharding import PartitionSpec as P

TILE = 128
CAP = 6


beta_one = 0.9
beta_two = 0.999
learn_rate = 0.02
eps_adam = 1e-08
bias_one = 1.0 - 0.9**10
bias_two = 1.0 - 0.999**10


def cast_kernel(order_ref, w_ref, copy_ref, half_ref):
    w = w_ref[...]
    copy_ref[...] = w
    half_ref[...] = w.astype(jnp.bfloat16)


def cast_weight(w, order):
    count = order.shape[0]
    depth, width = w.shape[0] // count, w.shape[1]
    blocks = w.reshape(count, depth, width)
    take = pl.BlockSpec((1, depth, width), lambda i, order: (order[i], 0, 0))
    put = pl.BlockSpec((1, depth, width), lambda i, order: (i, 0, 0))
    copied, half = pl.pallas_call(
        cast_kernel,
        out_shape=(
            jax.ShapeDtypeStruct(blocks.shape, jnp.float32),
            jax.ShapeDtypeStruct(blocks.shape, jnp.bfloat16),
        ),
        grid_spec=pltpu.PrefetchScalarGridSpec(
            num_scalar_prefetch=1, grid=(count,), in_specs=[take], out_specs=(take, put)
        ),
        cost_estimate=pl.CostEstimate(
            flops=w.size, bytes_accessed=10 * w.size, transcendentals=0
        ),
        name="cast_weight",
    )(order, blocks)
    return copied.reshape(w.shape), half


def copy_kernel(a_ref, b_ref, c_ref, d_ref):
    c_ref[...] = a_ref[...]
    d_ref[...] = b_ref[...]


def copy_pair(a, b):
    rows = a.shape[0] // 8
    spec = pl.BlockSpec((rows, a.shape[1]), lambda i: (i, 0))
    shape = jax.ShapeDtypeStruct(a.shape, a.dtype)
    return pl.pallas_call(
        copy_kernel,
        out_shape=(shape, shape),
        grid=(8,),
        in_specs=[spec, spec],
        out_specs=(spec, spec),
        cost_estimate=pl.CostEstimate(flops=0, bytes_accessed=16 * a.size, transcendentals=0),
        name="copy_pair",
    )(a, b)


def back_kernel(cot_ref, w_ref, out_ref):
    out_ref[0] = lax.dot_general(
        cot_ref[...], w_ref[0], (((1,), (1,)), ((), ())), preferred_element_type=jnp.float32
    ).astype(out_ref.dtype)


def back_product(cot, half, first, count, out_type):
    rows, width = cot.shape
    depth = half.shape[1]
    return pl.pallas_call(
        back_kernel,
        out_shape=jax.ShapeDtypeStruct((count, rows, depth), out_type),
        grid=(count,),
        in_specs=[
            pl.BlockSpec((rows, width), lambda i: (0, 0)),
            pl.BlockSpec((1, depth, width), lambda i: (i + first, 0, 0)),
        ],
        out_specs=pl.BlockSpec((1, rows, depth), lambda i: (i, 0, 0)),
        cost_estimate=pl.CostEstimate(
            flops=2 * count * rows * width * depth,
            bytes_accessed=count * depth * (2 * width + 4 * rows),
            transcendentals=0,
        ),
        name="back_product",
    )(cot, half)


def forward_kernel(x_ref, w_ref, out_ref):
    product = jnp.dot(x_ref[0], w_ref[0], preferred_element_type=jnp.float32)

    @pl.when(pl.program_id(0) == 0)
    def _():
        out_ref[...] = product

    @pl.when(pl.program_id(0) > 0)
    def _():
        out_ref[...] += product


def forward_product(x, half):
    count, rows, depth = x.shape
    width = half.shape[2]
    return pl.pallas_call(
        forward_kernel,
        out_shape=jax.ShapeDtypeStruct((rows, width), jnp.float32),
        grid=(count,),
        in_specs=[
            pl.BlockSpec((1, rows, depth), lambda i: (i, 0, 0)),
            pl.BlockSpec((1, depth, width), lambda i: (i, 0, 0)),
        ],
        out_specs=pl.BlockSpec((rows, width), lambda i: (0, 0)),
        cost_estimate=pl.CostEstimate(
            flops=2 * count * rows * width * depth,
            bytes_accessed=2 * count * depth * (rows + width),
            transcendentals=0,
        ),
        name="forward_product",
    )(x, half)


def tile_kernel(
    slots, owned, row, piece, lane, x_ref, cot_ref, w_in, m_in, v_in,
    w_out, m_out, v_out, fresh_ref, w_buf, m_buf, v_buf, load_sem, store_sem,
):
    parts = ((w_in, w_out, w_buf), (m_in, m_out, m_buf), (v_in, v_out, v_buf))

    def window(ref, i):
        return ref.at[
            pl.ds(pl.multiple_of(row[i] * TILE, TILE), TILE),
            pl.ds(pl.multiple_of(i // CAP * TILE, TILE), TILE),
        ]

    def load(i, k):
        source, _, buf = parts[k]
        return pltpu.make_async_copy(window(source, i), buf.at[i], load_sem.at[k, i])

    def store(i, k):
        _, target, buf = parts[k]
        return pltpu.make_async_copy(buf.at[i], window(target, i), store_sem.at[k, i])

    @pl.loop(0, slots)
    def _(i):
        @pl.when(owned[i] > 0)
        def _():
            for k in range(3):
                load(i, k).start()

    @pl.loop(0, slots)
    def _(i):
        @pl.when(owned[i] > 0)
        def _():
            x = x_ref[piece[i], :, pl.ds(pl.multiple_of(lane[i] * TILE, TILE), TILE)]
            cot = cot_ref[:, pl.ds(pl.multiple_of(i // CAP * TILE, TILE), TILE)]
            gradient = lax.dot_general(
                x, cot, (((0,), (0,)), ((), ())), preferred_element_type=jnp.float32
            )
            for k in range(3):
                load(i, k).wait()
            m = beta_one * m_buf[i] + (1.0 - beta_one) * gradient
            v = beta_two * v_buf[i] + (1.0 - beta_two) * gradient * gradient
            step = m / bias_one / (jnp.sqrt(v / bias_two) + eps_adam)
            w = w_buf[i] - learn_rate * step
            w_buf[i], m_buf[i], v_buf[i] = w, m, v
            fresh_ref[i] = w.astype(jnp.bfloat16)
            for k in range(3):
                store(i, k).start()

        @pl.when(owned[i] == 0)
        def _():
            fresh_ref[i] = jnp.zeros((TILE, TILE), jnp.bfloat16)

    @pl.loop(0, slots)
    def _(i):
        @pl.when(owned[i] > 0)
        def _():
            for k in range(3):
                store(i, k).wait()


def update_tiles(owned, row, piece, lane, x, cot, w, m, v):
    slots = owned.shape[0]
    smem = pl.BlockSpec(memory_space=pltpu.SMEM)
    vmem = pl.BlockSpec(memory_space=pltpu.VMEM)
    hbm = pl.BlockSpec(memory_space=pl.ANY)
    state = jax.ShapeDtypeStruct(w.shape, w.dtype)
    buf = pltpu.VMEM((slots, TILE, TILE), jnp.float32)
    return pl.pallas_call(
        functools.partial(tile_kernel, slots),
        out_shape=(
            state,
            state,
            state,
            jax.ShapeDtypeStruct((slots, TILE, TILE), jnp.bfloat16),
        ),
        in_specs=[smem] * 4 + [vmem] * 2 + [hbm] * 3,
        out_specs=(hbm, hbm, hbm, vmem),
        scratch_shapes=[buf, buf, buf]
        + [pltpu.SemaphoreType.DMA((3, slots)), pltpu.SemaphoreType.DMA((3, slots))],
        input_output_aliases={6: 0, 7: 1, 8: 2},
        cost_estimate=pl.CostEstimate(
            flops=2 * slots * TILE * TILE * cot.shape[0],
            bytes_accessed=26 * slots * TILE * TILE,
            transcendentals=slots * TILE * TILE,
        ),
        name="update_tiles",
    )(owned, row, piece, lane, x, cot, w, m, v)


def swap(a, axis, size, bit):
    return lax.ppermute(a, axis, [(i, i ^ bit) for i in range(size)])


def owned_slots(tile_mask, group_at, shard_at, row_tiles, col_tiles):
    mask_cols = lax.dynamic_slice_in_dim(tile_mask, shard_at * col_tiles, col_tiles, 1)
    count = tile_mask.shape[0]
    at = jnp.arange(count)
    before = (at[None, :] < at[:, None]).astype(jnp.float32)
    rank = jnp.dot(before, mask_cols.astype(jnp.float32)).astype(jnp.int32)
    hit = (mask_cols[:, :, None] > 0) & (rank[:, :, None] == jnp.arange(CAP)[None, None, :])
    row = jnp.sum(jnp.where(hit, at[:, None, None], 0), axis=0).reshape(-1)
    live = jnp.sum(hit.astype(jnp.int32), axis=0).reshape(-1)
    owned = jnp.where(row // row_tiles == group_at, live, 0)
    return owned, row - group_at * row_tiles


def pair_shards(groups, shard_count, rollout_rows, assign, cotangent, w_master, adam_m, adam_v, tile_mask):
    group_at = lax.axis_index("group")
    shard_at = lax.axis_index("shard")
    row_count, features = rollout_rows.shape
    width = cotangent.shape[1]
    col_tiles = width // TILE
    row_tiles = w_master.shape[0] // TILE
    half_count = shard_count // 2
    bits = [half_count >> (k + 1) for k in range(half_count.bit_length() - 1)]
    offsets = [0]
    for bit in bits:
        offsets = offsets + [o | bit for o in offsets]
    base = shard_at % half_count
    order = base ^ jnp.asarray(offsets, jnp.int32)
    in_half = shard_at // half_count == group_at

    far = swap(rollout_rows, "shard", shard_count, half_count)
    cot_other = swap(cotangent, "group", groups, 1)
    keep = jnp.where(in_half, rollout_rows, far)
    give = jnp.where(in_half, far, rollout_rows)
    x_parts = [keep, swap(give, "group", groups, 1)]
    for bit in bits:
        x_parts = x_parts + [swap(a, "shard", shard_count, bit) for a in x_parts]

    w_copy, half = cast_weight(w_master, order)
    m_copy, v_copy = copy_pair(adam_m, adam_v)

    cot_rel = jnp.concatenate([cotangent, cot_other], axis=0)
    left = half_count // 2
    kept = back_product(cot_rel, half, 0, left, jnp.float32)
    sent = back_product(cot_rel, half, left, left, jnp.bfloat16)
    for bit in reversed(bits):
        total = kept + swap(sent, "shard", shard_count, bit).astype(jnp.float32)
        left //= 2
        if left:
            kept, sent = total[:left], total[left:].astype(jnp.bfloat16)
    total = total.reshape(groups, row_count, features)
    other = swap(total[1].astype(jnp.bfloat16), "group", groups, 1).astype(jnp.float32)
    near = jnp.where(in_half, total[0], other)
    away = jnp.where(in_half, other, total[0]).astype(jnp.bfloat16)
    back = swap(away, "shard", shard_count, half_count).astype(jnp.float32)
    input_grad = (near + back).astype(jnp.bfloat16)

    row_total = groups * row_count
    turned = jnp.roll(assign, -group_at * row_count)
    turned = lax.rem(turned + row_total - group_at * row_count, row_total)
    pick = (jnp.arange(row_total)[:, None] == turned[None, :]).astype(jnp.bfloat16)
    cot_turned = jnp.dot(pick, cot_rel, preferred_element_type=jnp.float32).astype(jnp.bfloat16)

    x_all = jnp.stack(x_parts).reshape(half_count, row_total, features)
    partial = forward_product(x_all, half)
    give = jnp.take(partial, turned[row_count:], axis=0).astype(jnp.bfloat16)
    mine = jnp.take(partial, turned[:row_count], axis=0)
    projected = (mine + swap(give, "group", groups, 1).astype(jnp.float32)).astype(jnp.bfloat16)

    owned, row = owned_slots(tile_mask, group_at, shard_at, row_tiles, col_tiles)
    per_block = features // TILE
    block = jnp.clip(row // per_block, 0, half_count - 1) ^ base
    piece = jnp.argmax(block[:, None] == jnp.asarray(offsets)[None, :], axis=1)
    lane = lax.rem(row + row_tiles * groups, per_block)
    w_updated, m_updated, v_updated, fresh = update_tiles(
        owned, row, piece.astype(jnp.int32), lane, x_all, cot_turned, w_copy, m_copy, v_copy
    )
    tiles = fresh + swap(fresh, "group", groups, 1)
    rollout_tiles = tiles.reshape(col_tiles, CAP, TILE, TILE)
    return (projected, input_grad, w_updated, m_updated, v_updated, rollout_tiles)


def any_shards(groups, shard_count, rollout_rows, assign, cotangent, w_master, adam_m, adam_v, tile_mask):
    group_at = lax.axis_index("group")
    shard_at = lax.axis_index("shard")
    row_count, features = rollout_rows.shape
    width = cotangent.shape[1]
    col_tiles = width // TILE
    row_tiles = w_master.shape[0] // TILE
    depth = w_master.shape[0]
    per_group = shard_count // groups
    row_total = groups * row_count
    order = jnp.arange(per_group, dtype=jnp.int32)
    w_copy, half = cast_weight(w_master, order)
    m_copy, v_copy = copy_pair(adam_m, adam_v)
    x_cols = lax.all_gather(rollout_rows, "group", axis=0, tiled=True)
    x_full = lax.all_gather(x_cols, "shard", axis=0)
    x_all = lax.dynamic_slice_in_dim(x_full, group_at * per_group, per_group, 0)
    cot_all = lax.all_gather(cotangent, "group", axis=0, tiled=True)
    products = back_product(cot_all, half, 0, per_group, jnp.bfloat16)
    products = products.reshape(per_group, groups, row_count, features)
    products = products.transpose(1, 0, 2, 3).reshape(shard_count * row_count, features)
    summed = lax.psum_scatter(products, "shard", scatter_dimension=0, tiled=True)
    moves = [
        (g * shard_count + r * per_group + k, r * shard_count + g * per_group + k)
        for g in range(groups)
        for r in range(groups)
        for k in range(per_group)
    ]
    input_grad = lax.ppermute(summed, ("group", "shard"), moves)
    pick = (jnp.arange(row_total)[:, None] == assign[None, :]).astype(jnp.bfloat16)
    cot_turned = jnp.dot(pick, cot_all, preferred_element_type=jnp.float32).astype(jnp.bfloat16)
    partial = jnp.take(forward_product(x_all, half), assign, axis=0)
    projected = lax.psum_scatter(partial, "group", scatter_dimension=0, tiled=True)
    projected = projected.astype(jnp.bfloat16)
    owned, row = owned_slots(tile_mask, group_at, shard_at, row_tiles, col_tiles)
    per_block = features // TILE
    piece = jnp.clip(row // per_block, 0, per_group - 1)
    lane = lax.rem(row + row_tiles * groups, per_block)
    w_updated, m_updated, v_updated, fresh = update_tiles(
        owned, row, piece, lane, x_all, cot_turned, w_copy, m_copy, v_copy
    )
    rollout_tiles = lax.psum(fresh, "group").reshape(col_tiles, CAP, TILE, TILE)
    return (projected, input_grad, w_updated, m_updated, v_updated, rollout_tiles)


def solution(mesh):
    groups, shard_count = mesh.shape["group"], mesh.shape["shard"]
    paired = groups == 2 and shard_count >= 4 and shard_count & (shard_count - 1) == 0
    body = functools.partial(pair_shards if paired else any_shards, groups, shard_count)
    placed = (
        P("group", "shard"),
        P(),
        P("group", "shard"),
        P("group", "shard"),
        P("group", "shard"),
        P("group", "shard"),
        P(),
    )
    return jax.shard_map(
        body,
        mesh=mesh,
        in_specs=placed,
        out_specs=(
            P("group", "shard"),
            P("group", "shard"),
            P("group", "shard"),
            P("group", "shard"),
            P("group", "shard"),
            P("shard", None, None, None),
        ),
        check_vma=False,
    )
```

```python
import functools

import jax
import jax.numpy as jnp
from jax import lax
from jax.experimental import pallas as pl
from jax.experimental.pallas import tpu as pltpu
from jax.sharding import PartitionSpec as P

TILE = 128
CAP = 6


beta_one = 0.9
beta_two = 0.999
learn_rate = 0.02
eps_adam = 1e-08
bias_one = 1.0 - 0.9**10
bias_two = 1.0 - 0.999**10


def cast_kernel(order_ref, w_ref, copy_ref, half_ref):
    w = w_ref[...]
    copy_ref[...] = w
    half_ref[...] = w.astype(jnp.bfloat16)


def cast_weight(w, order):
    count = order.shape[0]
    depth, width = w.shape[0] // count, w.shape[1]
    blocks = w.reshape(count, depth, width)
    take = pl.BlockSpec((1, depth, width), lambda i, order: (order[i], 0, 0))
    put = pl.BlockSpec((1, depth, width), lambda i, order: (i, 0, 0))
    copied, half = pl.pallas_call(
        cast_kernel,
        out_shape=(
            jax.ShapeDtypeStruct(blocks.shape, jnp.float32),
            jax.ShapeDtypeStruct(blocks.shape, jnp.bfloat16),
        ),
        grid_spec=pltpu.PrefetchScalarGridSpec(
            num_scalar_prefetch=1, grid=(count,), in_specs=[take], out_specs=(take, put)
        ),
        cost_estimate=pl.CostEstimate(
            flops=w.size, bytes_accessed=10 * w.size, transcendentals=0
        ),
        name="cast_weight",
    )(order, blocks)
    return copied.reshape(w.shape), half


def copy_kernel(a_ref, c_ref):
    c_ref[...] = a_ref[...]


def copy_state(a):
    rows = a.shape[0] // 8
    spec = pl.BlockSpec((rows, a.shape[1]), lambda i: (i, 0))
    return pl.pallas_call(
        copy_kernel,
        out_shape=jax.ShapeDtypeStruct(a.shape, a.dtype),
        grid=(8,),
        in_specs=[spec],
        out_specs=spec,
        cost_estimate=pl.CostEstimate(flops=0, bytes_accessed=8 * a.size, transcendentals=0),
        name="copy_state",
    )(a)


def first_kernel(order, cot_ref, w_ref, copy_ref, half_ref, out_ref):
    w = w_ref[0]
    copy_ref[0] = w
    half = w.astype(jnp.bfloat16)
    half_ref[0] = half
    out_ref[0] = lax.dot_general(
        cot_ref[...], half, (((1,), (1,)), ((), ())), preferred_element_type=jnp.float32
    ).astype(out_ref.dtype)


def second_kernel(order, cot_ref, w_ref, _, copy_ref, half_ref, out_ref):
    first_kernel(order, cot_ref, w_ref, copy_ref, half_ref, out_ref)


def weight_pass(cot, blocks, order, out_type, copied=None):
    count = order.shape[0]
    rows, width = cot.shape
    depth = blocks.shape[1]
    whole = pl.BlockSpec((rows, width), lambda i, order: (0, 0))
    take = pl.BlockSpec((1, depth, width), lambda i, order: (order[i], 0, 0))
    put = pl.BlockSpec((1, depth, width), lambda i, order: (i, 0, 0))
    out = pl.BlockSpec((1, rows, depth), lambda i, order: (i, 0, 0))
    again = copied is not None
    return pl.pallas_call(
        second_kernel if again else first_kernel,
        out_shape=(
            jax.ShapeDtypeStruct(blocks.shape, jnp.float32),
            jax.ShapeDtypeStruct((count, depth, width), jnp.bfloat16),
            jax.ShapeDtypeStruct((count, rows, depth), out_type),
        ),
        grid_spec=pltpu.PrefetchScalarGridSpec(
            num_scalar_prefetch=1,
            grid=(count,),
            in_specs=[whole, take] + [pl.BlockSpec(memory_space=pl.ANY)] * again,
            out_specs=(take, put, out),
        ),
        input_output_aliases={3: 0} if again else {},
        cost_estimate=pl.CostEstimate(
            flops=2 * count * rows * width * depth,
            bytes_accessed=count * depth * (10 * width + 4 * rows),
            transcendentals=0,
        ),
        name="weight_pass",
    )(order, cot, blocks, *([copied] if again else []))


def back_kernel(cot_ref, w_ref, out_ref):
    out_ref[0] = lax.dot_general(
        cot_ref[...], w_ref[0], (((1,), (1,)), ((), ())), preferred_element_type=jnp.float32
    ).astype(out_ref.dtype)


def back_product(cot, half, first, count, out_type):
    rows, width = cot.shape
    depth = half.shape[1]
    return pl.pallas_call(
        back_kernel,
        out_shape=jax.ShapeDtypeStruct((count, rows, depth), out_type),
        grid=(count,),
        in_specs=[
            pl.BlockSpec((rows, width), lambda i: (0, 0)),
            pl.BlockSpec((1, depth, width), lambda i: (i + first, 0, 0)),
        ],
        out_specs=pl.BlockSpec((1, rows, depth), lambda i: (i, 0, 0)),
        cost_estimate=pl.CostEstimate(
            flops=2 * count * rows * width * depth,
            bytes_accessed=count * depth * (2 * width + 4 * rows),
            transcendentals=0,
        ),
        name="back_product",
    )(cot, half)


def forward_kernel(x_ref, w_ref, out_ref):
    product = jnp.dot(x_ref[0], w_ref[0], preferred_element_type=jnp.float32)

    @pl.when(pl.program_id(0) == 0)
    def _():
        out_ref[...] = product

    @pl.when(pl.program_id(0) > 0)
    def _():
        out_ref[...] += product


def forward_product(x, half):
    count, rows, depth = x.shape
    width = half.shape[2]
    return pl.pallas_call(
        forward_kernel,
        out_shape=jax.ShapeDtypeStruct((rows, width), jnp.float32),
        grid=(count,),
        in_specs=[
            pl.BlockSpec((1, rows, depth), lambda i: (i, 0, 0)),
            pl.BlockSpec((1, depth, width), lambda i: (i, 0, 0)),
        ],
        out_specs=pl.BlockSpec((rows, width), lambda i: (0, 0)),
        cost_estimate=pl.CostEstimate(
            flops=2 * count * rows * width * depth,
            bytes_accessed=2 * count * depth * (rows + width),
            transcendentals=0,
        ),
        name="forward_product",
    )(x, half)


def pieces_kernel(count, *refs):
    x_refs, w_ref, refs = refs[: 2 * count], refs[2 * count], refs[2 * count + 1 :]
    out_ref = refs[-1]
    rows = x_refs[0].shape[0]
    for side in range(2):
        into = pl.ds(side * rows, rows)
        for n in range(count):
            product = jnp.dot(
                x_refs[2 * n + side][...], w_ref[n], preferred_element_type=jnp.float32
            )
            if n > 0:
                out_ref[into, :] += product
            elif len(refs) > 1:
                out_ref[into, :] = refs[0][into, :] + product
            else:
                out_ref[into, :] = product


def pieces_product(parts, half, base=None):
    count = half.shape[0]
    rows, depth = parts[0].shape
    width = half.shape[2]
    more = [] if base is None else [base]
    return pl.pallas_call(
        functools.partial(pieces_kernel, count),
        out_shape=jax.ShapeDtypeStruct((2 * rows, width), jnp.float32),
        in_specs=[pl.BlockSpec(memory_space=pltpu.VMEM)] * (2 * count + 1 + len(more)),
        out_specs=pl.BlockSpec(memory_space=pltpu.VMEM),
        cost_estimate=pl.CostEstimate(
            flops=4 * count * rows * width * depth,
            bytes_accessed=2 * count * depth * (2 * rows + width),
            transcendentals=0,
        ),
        name="pieces_product",
    )(*parts, half, *more)


def tile_kernel(slots, count, sides, owned, row, piece, lane, *refs):
    x_refs = refs[: count * sides]
    (
        cot_ref, w_in, m_in, v_in, w_out, m_out, v_out, fresh_ref,
        w_buf, m_buf, v_buf, x_buf, load_sem, x_sem, store_sem,
    ) = refs[count * sides :]
    parts = ((w_in, w_out, w_buf), (m_in, m_out, m_buf), (v_in, v_out, v_buf))
    rows = x_refs[0].shape[0]

    def window(ref, i):
        return ref.at[
            pl.ds(pl.multiple_of(row[i] * TILE, TILE), TILE),
            pl.ds(pl.multiple_of(i // CAP * TILE, TILE), TILE),
        ]

    def load(i, k):
        source, _, buf = parts[k]
        return pltpu.make_async_copy(window(source, i), buf.at[i], load_sem.at[k, i])

    def store(i, k):
        _, target, buf = parts[k]
        return pltpu.make_async_copy(buf.at[i], window(target, i), store_sem.at[k, i])

    def fetch(i, n, side):
        return pltpu.make_async_copy(
            x_refs[n * sides + side].at[:, pl.ds(pl.multiple_of(lane[i] * TILE, TILE), TILE)],
            x_buf.at[i, pl.ds(side * rows, rows), :],
            x_sem.at[side, i],
        )

    @pl.loop(0, slots)
    def _(i):
        @pl.when(owned[i] > 0)
        def _():
            for n in range(count):

                @pl.when(piece[i] == n)
                def _():
                    for side in range(sides):
                        fetch(i, n, side).start()

            for k in range(3):
                load(i, k).start()

    @pl.loop(0, slots)
    def _(i):
        @pl.when(owned[i] > 0)
        def _():
            for side in range(sides):
                fetch(i, 0, side).wait()
            cot = cot_ref[:, pl.ds(pl.multiple_of(i // CAP * TILE, TILE), TILE)]
            gradient = lax.dot_general(
                x_buf[i], cot, (((0,), (0,)), ((), ())), preferred_element_type=jnp.float32
            )
            for k in range(3):
                load(i, k).wait()
            m = beta_one * m_buf[i] + (1.0 - beta_one) * gradient
            v = beta_two * v_buf[i] + (1.0 - beta_two) * gradient * gradient
            step = m / bias_one / (jnp.sqrt(v / bias_two) + eps_adam)
            w = w_buf[i] - learn_rate * step
            w_buf[i], m_buf[i], v_buf[i] = w, m, v
            fresh_ref[i] = w.astype(jnp.bfloat16)
            for k in range(3):
                store(i, k).start()

        @pl.when(owned[i] == 0)
        def _():
            fresh_ref[i] = jnp.zeros((TILE, TILE), jnp.bfloat16)

    @pl.loop(0, slots)
    def _(i):
        @pl.when(owned[i] > 0)
        def _():
            for k in range(3):
                store(i, k).wait()


def update_tiles(owned, row, piece, lane, x_parts, count, cot, w, m, v):
    slots = owned.shape[0]
    sides = len(x_parts) // count
    smem = pl.BlockSpec(memory_space=pltpu.SMEM)
    vmem = pl.BlockSpec(memory_space=pltpu.VMEM)
    hbm = pl.BlockSpec(memory_space=pl.ANY)
    state = jax.ShapeDtypeStruct(w.shape, w.dtype)
    buf = pltpu.VMEM((slots, TILE, TILE), jnp.float32)
    sems = pltpu.SemaphoreType.DMA((3, slots))
    first = 5 + len(x_parts)
    return pl.pallas_call(
        functools.partial(tile_kernel, slots, count, sides),
        out_shape=(
            state,
            state,
            state,
            jax.ShapeDtypeStruct((slots, TILE, TILE), jnp.bfloat16),
        ),
        in_specs=[smem] * 4 + [hbm] * len(x_parts) + [vmem] + [hbm] * 3,
        out_specs=(hbm, hbm, hbm, vmem),
        scratch_shapes=[buf, buf, buf, pltpu.VMEM((slots, cot.shape[0], TILE), jnp.bfloat16)]
        + [sems, pltpu.SemaphoreType.DMA((sides, slots)), sems],
        input_output_aliases={first: 0, first + 1: 1, first + 2: 2},
        cost_estimate=pl.CostEstimate(
            flops=2 * slots * TILE * TILE * cot.shape[0],
            bytes_accessed=26 * slots * TILE * TILE,
            transcendentals=slots * TILE * TILE,
        ),
        name="update_tiles",
    )(owned, row, piece, lane, *x_parts, cot, w, m, v)


def swap(a, axis, size, bit):
    return lax.ppermute(a, axis, [(i, i ^ bit) for i in range(size)])


def owned_slots(tile_mask, group_at, shard_at, row_tiles, col_tiles):
    mask_cols = lax.dynamic_slice_in_dim(tile_mask, shard_at * col_tiles, col_tiles, 1)
    count = tile_mask.shape[0]
    at = jnp.arange(count)
    before = (at[None, :] < at[:, None]).astype(jnp.float32)
    rank = jnp.dot(before, mask_cols.astype(jnp.float32)).astype(jnp.int32)
    hit = (mask_cols[:, :, None] > 0) & (rank[:, :, None] == jnp.arange(CAP)[None, None, :])
    row = jnp.sum(jnp.where(hit, at[:, None, None], 0), axis=0).reshape(-1)
    live = jnp.sum(hit.astype(jnp.int32), axis=0).reshape(-1)
    owned = jnp.where(row // row_tiles == group_at, live, 0)
    return owned, row - group_at * row_tiles


def pair_shards(groups, shard_count, rollout_rows, assign, cotangent, w_master, adam_m, adam_v, tile_mask):
    group_at = lax.axis_index("group")
    shard_at = lax.axis_index("shard")
    row_count, features = rollout_rows.shape
    width = cotangent.shape[1]
    col_tiles = width // TILE
    row_tiles = w_master.shape[0] // TILE
    half_count = shard_count // 2
    bits = [half_count >> (k + 1) for k in range(half_count.bit_length() - 1)]
    offsets = [0]
    for bit in bits:
        offsets = offsets + [o | bit for o in offsets]
    base = shard_at % half_count
    order = base ^ jnp.asarray(offsets, jnp.int32)
    in_half = shard_at // half_count == group_at

    scope = jax.named_scope
    blocks = w_master.reshape(half_count, features, width)
    low = half_count // 2

    with scope("cot"):
        cot_other = swap(cotangent, "group", groups, 1)
    with scope("far"):
        far = swap(rollout_rows, "shard", shard_count, half_count)
    with scope("copy_m"):
        m_copy = copy_state(adam_m)
    cot_rel = jnp.concatenate([cotangent, cot_other], axis=0)
    with scope("pass_one"):
        w_copy, half_high, sent = weight_pass(cot_rel, blocks, order[low:], jnp.bfloat16)
    with scope("core_sum"):
        got = swap(sent, "shard", shard_count, bits[-1])
    keep = jnp.where(in_half, rollout_rows, far)
    give = jnp.where(in_half, far, rollout_rows)
    with scope("cross"):
        x_parts = [keep, swap(give, "group", groups, 1)]
    for k, bit in enumerate(bits):
        held = list(x_parts)
        for j, part in enumerate(held):
            with scope(f"gather_{k}_{j}"):
                x_parts.append(swap(part, "shard", shard_count, bit))

    with scope("pass_two"):
        w_copy, half_low, kept = weight_pass(cot_rel, blocks, order[:low], jnp.float32, w_copy)
    with scope("copy_v"):
        v_copy = copy_state(adam_v)
    sums = [
        [
            kept[n, r * row_count : (r + 1) * row_count]
            + got[n, r * row_count : (r + 1) * row_count].astype(jnp.float32)
            for r in range(2)
        ]
        for n in range(low)
    ]
    done = [None, None]
    for r in (1, 0):
        terms = {o: sums[n][r] for n, o in enumerate(offsets[:low])}
        for k, bit in enumerate(bits[:-1]):
            for o in sorted([o for o in terms if o & bit], reverse=True):
                with scope(f"sum_{k}_{r}_{o}"):
                    term = terms.pop(o).astype(jnp.bfloat16)
                    term = swap(term, "shard", shard_count, bit)
                terms[o ^ bit] = terms[o ^ bit] + term.astype(jnp.float32)
        done[r] = terms[0]
    with scope("cross_sum"):
        other = swap(done[1].astype(jnp.bfloat16), "group", groups, 1).astype(jnp.float32)
    near = jnp.where(in_half, done[0], other)
    away = jnp.where(in_half, other, done[0]).astype(jnp.bfloat16)
    with scope("far_sum"):
        back = swap(away, "shard", shard_count, half_count).astype(jnp.float32)
    input_grad = (near + back).astype(jnp.bfloat16)

    row_total = groups * row_count
    turned = jnp.roll(assign, -group_at * row_count)
    turned = lax.rem(turned + row_total - group_at * row_count, row_total)
    pick = (jnp.arange(row_total)[:, None] == turned[None, :]).astype(jnp.bfloat16)
    cot_turned = jnp.dot(pick, cot_rel, preferred_element_type=jnp.float32).astype(jnp.bfloat16)

    owned, row = owned_slots(tile_mask, group_at, shard_at, row_tiles, col_tiles)
    per_block = features // TILE
    block = jnp.clip(row // per_block, 0, half_count - 1) ^ base
    piece = jnp.argmax(block[:, None] == jnp.asarray(offsets)[None, :], axis=1)
    lane = lax.rem(row + row_tiles * groups, per_block)
    with scope("update"):
        w_updated, m_updated, v_updated, fresh = update_tiles(
            owned, row, piece.astype(jnp.int32), lane, x_parts, half_count, cot_turned,
            w_copy.reshape(w_master.shape), m_copy, v_copy,
        )
    with scope("tiles"):
        tiles = fresh + swap(fresh, "group", groups, 1)
    rollout_tiles = tiles.reshape(col_tiles, CAP, TILE, TILE)

    with scope("product_low"):
        partial = pieces_product(x_parts[: 2 * low], half_low)
    with scope("product_high"):
        partial = pieces_product(x_parts[2 * low :], half_high, partial)
    give = jnp.take(partial, turned[row_count:], axis=0).astype(jnp.bfloat16)
    mine = jnp.take(partial, turned[:row_count], axis=0)
    with scope("forward"):
        taken = swap(give, "group", groups, 1).astype(jnp.float32)
    projected = (mine + taken).astype(jnp.bfloat16)
    return (projected, input_grad, w_updated, m_updated, v_updated, rollout_tiles)


def any_shards(groups, shard_count, rollout_rows, assign, cotangent, w_master, adam_m, adam_v, tile_mask):
    group_at = lax.axis_index("group")
    shard_at = lax.axis_index("shard")
    row_count, features = rollout_rows.shape
    width = cotangent.shape[1]
    col_tiles = width // TILE
    row_tiles = w_master.shape[0] // TILE
    depth = w_master.shape[0]
    per_group = shard_count // groups
    row_total = groups * row_count
    order = jnp.arange(per_group, dtype=jnp.int32)
    w_copy, half = cast_weight(w_master, order)
    m_copy, v_copy = copy_state(adam_m), copy_state(adam_v)
    x_cols = lax.all_gather(rollout_rows, "group", axis=0, tiled=True)
    x_full = lax.all_gather(x_cols, "shard", axis=0)
    x_all = lax.dynamic_slice_in_dim(x_full, group_at * per_group, per_group, 0)
    cot_all = lax.all_gather(cotangent, "group", axis=0, tiled=True)
    products = back_product(cot_all, half, 0, per_group, jnp.bfloat16)
    products = products.reshape(per_group, groups, row_count, features)
    products = products.transpose(1, 0, 2, 3).reshape(shard_count * row_count, features)
    summed = lax.psum_scatter(products, "shard", scatter_dimension=0, tiled=True)
    moves = [
        (g * shard_count + r * per_group + k, r * shard_count + g * per_group + k)
        for g in range(groups)
        for r in range(groups)
        for k in range(per_group)
    ]
    input_grad = lax.ppermute(summed, ("group", "shard"), moves)
    pick = (jnp.arange(row_total)[:, None] == assign[None, :]).astype(jnp.bfloat16)
    cot_turned = jnp.dot(pick, cot_all, preferred_element_type=jnp.float32).astype(jnp.bfloat16)
    partial = jnp.take(forward_product(x_all, half), assign, axis=0)
    projected = lax.psum_scatter(partial, "group", scatter_dimension=0, tiled=True)
    projected = projected.astype(jnp.bfloat16)
    owned, row = owned_slots(tile_mask, group_at, shard_at, row_tiles, col_tiles)
    per_block = features // TILE
    piece = jnp.clip(row // per_block, 0, per_group - 1)
    lane = lax.rem(row + row_tiles * groups, per_block)
    w_updated, m_updated, v_updated, fresh = update_tiles(
        owned, row, piece, lane, list(x_all), per_group, cot_turned, w_copy, m_copy, v_copy
    )
    rollout_tiles = lax.psum(fresh, "group").reshape(col_tiles, CAP, TILE, TILE)
    return (projected, input_grad, w_updated, m_updated, v_updated, rollout_tiles)


def solution(mesh):
    groups, shard_count = mesh.shape["group"], mesh.shape["shard"]
    paired = groups == 2 and shard_count >= 4 and shard_count & (shard_count - 1) == 0
    body = functools.partial(pair_shards if paired else any_shards, groups, shard_count)
    placed = (
        P("group", "shard"),
        P(),
        P("group", "shard"),
        P("group", "shard"),
        P("group", "shard"),
        P("group", "shard"),
        P(),
    )
    return jax.shard_map(
        body,
        mesh=mesh,
        in_specs=placed,
        out_specs=(
            P("group", "shard"),
            P("group", "shard"),
            P("group", "shard"),
            P("group", "shard"),
            P("group", "shard"),
            P("shard", None, None, None),
        ),
        check_vma=False,
    )
```

```python
import functools

import jax
import jax.numpy as jnp
from jax import lax
from jax.experimental import pallas as pl
from jax.experimental.pallas import tpu as pltpu
from jax.sharding import PartitionSpec as P


TILE = 128
CAP = 6


beta_one = 0.9
beta_two = 0.999
learn_rate = 0.02
eps_adam = 1e-08
bias_one = 1.0 - 0.9**10
bias_two = 1.0 - 0.999**10


def cast_kernel(order, w_ref, *refs):
    copy_ref, half_ref = refs[-2:]
    w = w_ref[...]
    copy_ref[...] = w
    half_ref[...] = w.astype(jnp.bfloat16)


def cast_pass(blocks, order, first=0, after=()):
    count = order.shape[0] - first
    _, depth, width = blocks.shape
    take = pl.BlockSpec((1, depth, width), lambda i, order: (order[i + first], 0, 0))
    put = pl.BlockSpec((1, depth, width), lambda i, order: (i, 0, 0))
    return pl.pallas_call(
        cast_kernel,
        out_shape=(
            jax.ShapeDtypeStruct(blocks.shape, jnp.float32),
            jax.ShapeDtypeStruct((count, depth, width), jnp.bfloat16),
        ),
        grid_spec=pltpu.PrefetchScalarGridSpec(
            num_scalar_prefetch=1,
            grid=(count,),
            in_specs=[take] + [pl.BlockSpec(memory_space=pl.ANY)] * len(after),
            out_specs=(take, put),
        ),
        cost_estimate=pl.CostEstimate(
            flops=0, bytes_accessed=10 * count * depth * width, transcendentals=0
        ),
        name="cast_pass",
    )(order, blocks, *after)


def back_kernel(near_ref, other_ref, half_ref, out_ref, cot_ref):
    rows = near_ref.shape[0]

    @pl.when(pl.program_id(0) == 0)
    def _():
        cot_ref[:rows, :] = near_ref[...]
        cot_ref[rows:, :] = other_ref[...]

    out_ref[0] = lax.dot_general(
        cot_ref[...], half_ref[0], (((1,), (1,)), ((), ())), preferred_element_type=jnp.float32
    ).astype(out_ref.dtype)


def back_product(near, other, half):
    count, depth, width = half.shape
    rows = near.shape[0] + other.shape[0]
    vmem = pl.BlockSpec(memory_space=pltpu.VMEM)
    return pl.pallas_call(
        back_kernel,
        out_shape=jax.ShapeDtypeStruct((count, rows, depth), jnp.bfloat16),
        grid=(count,),
        in_specs=[vmem, vmem, pl.BlockSpec((1, depth, width), lambda i: (i, 0, 0))],
        out_specs=pl.BlockSpec((1, rows, depth), lambda i: (i, 0, 0)),
        scratch_shapes=[pltpu.VMEM((rows, width), jnp.bfloat16)],
        cost_estimate=pl.CostEstimate(
            flops=2 * count * rows * width * depth,
            bytes_accessed=2 * count * depth * (width + rows),
            transcendentals=0,
        ),
        name="back_product",
    )(near, other, half)


def weight_kernel(
    order, near_ref, other_ref, w_ref, _, copy_ref, half_ref, out_ref, cot_ref
):
    rows = near_ref.shape[0]

    @pl.when(pl.program_id(0) == 0)
    def _():
        cot_ref[:rows, :] = near_ref[...]
        cot_ref[rows:, :] = other_ref[...]

    w = w_ref[0]
    copy_ref[0] = w
    half = w.astype(jnp.bfloat16)
    half_ref[0] = half
    out_ref[0] = lax.dot_general(
        cot_ref[...], half, (((1,), (1,)), ((), ())), preferred_element_type=jnp.float32
    ).astype(out_ref.dtype)


def turn_kernel(near_ref, other_ref, turn_ref, out_ref):
    rows = near_ref.shape[0]
    place = lax.broadcasted_iota(jnp.int32, (2 * rows, 2 * rows), 0)
    chosen = (place == turn_ref[...]).astype(jnp.bfloat16)
    cot = jnp.concatenate([near_ref[...], other_ref[...]], axis=0)
    out_ref[...] = jnp.dot(chosen, cot, preferred_element_type=jnp.float32).astype(jnp.bfloat16)


def turn_rows(near, other, turn):
    rows, width = near.shape
    vmem = pl.BlockSpec(memory_space=pltpu.VMEM)
    return pl.pallas_call(
        turn_kernel,
        out_shape=jax.ShapeDtypeStruct((2 * rows, width), jnp.bfloat16),
        in_specs=[vmem] * 3,
        out_specs=vmem,
        cost_estimate=pl.CostEstimate(
            flops=8 * rows * rows * width, bytes_accessed=8 * rows * width, transcendentals=0
        ),
        name="turn_rows",
    )(near, other, turn)


def weight_pass(near, other, blocks, order, count, copied):
    width = near.shape[1]
    rows = near.shape[0] + other.shape[0]
    depth = blocks.shape[1]
    vmem = pl.BlockSpec(memory_space=pltpu.VMEM)
    take = pl.BlockSpec((1, depth, width), lambda i, order: (order[i], 0, 0))
    put = pl.BlockSpec((1, depth, width), lambda i, order: (i, 0, 0))
    out = pl.BlockSpec((1, rows, depth), lambda i, order: (i, 0, 0))
    return pl.pallas_call(
        weight_kernel,
        out_shape=(
            jax.ShapeDtypeStruct(blocks.shape, jnp.float32),
            jax.ShapeDtypeStruct((count, depth, width), jnp.bfloat16),
            jax.ShapeDtypeStruct((count, rows, depth), jnp.bfloat16),
        ),
        grid_spec=pltpu.PrefetchScalarGridSpec(
            num_scalar_prefetch=1,
            grid=(count,),
            in_specs=[vmem, vmem, take, pl.BlockSpec(memory_space=pl.ANY)],
            out_specs=(take, put, out),
            scratch_shapes=[pltpu.VMEM((rows, width), jnp.bfloat16)],
        ),
        input_output_aliases={4: 0},
        cost_estimate=pl.CostEstimate(
            flops=2 * count * rows * width * depth,
            bytes_accessed=count * depth * (10 * width + 2 * rows),
            transcendentals=0,
        ),
        name="weight_pass",
    )(order, near, other, blocks, copied)


def forward_kernel(x_ref, w_ref, out_ref):
    product = jnp.dot(x_ref[0], w_ref[0], preferred_element_type=jnp.float32)

    @pl.when(pl.program_id(0) == 0)
    def _():
        out_ref[...] = product

    @pl.when(pl.program_id(0) > 0)
    def _():
        out_ref[...] += product


def forward_product(x, half):
    count, rows, depth = x.shape
    width = half.shape[2]
    return pl.pallas_call(
        forward_kernel,
        out_shape=jax.ShapeDtypeStruct((rows, width), jnp.float32),
        grid=(count,),
        in_specs=[
            pl.BlockSpec((1, rows, depth), lambda i: (i, 0, 0)),
            pl.BlockSpec((1, depth, width), lambda i: (i, 0, 0)),
        ],
        out_specs=pl.BlockSpec((rows, width), lambda i: (0, 0)),
        cost_estimate=pl.CostEstimate(
            flops=2 * count * rows * width * depth,
            bytes_accessed=2 * count * depth * (rows + width),
            transcendentals=0,
        ),
        name="forward_product",
    )(x, half)


def tile_kernel(slots, count, sides, owned, row, piece, lane, *refs):
    x_refs = refs[: count * sides]
    (
        cot_ref, w_in, m_in, v_in, w_out, m_out, v_out, fresh_ref,
        w_buf, m_buf, v_buf, x_buf, load_sem, x_sem, store_sem,
    ) = refs[count * sides :]
    parts = ((w_in, w_buf), (m_in, m_buf), (v_in, v_buf))
    rows = x_refs[0].shape[0]

    def window(ref, i):
        return ref.at[
            pl.ds(pl.multiple_of(row[i] * TILE, TILE), TILE),
            pl.ds(pl.multiple_of(i // CAP * TILE, TILE), TILE),
        ]

    def load(i, k):
        source, buf = parts[k]
        return pltpu.make_async_copy(window(source, i), buf.at[i], load_sem.at[k, i])

    def store(i, k):
        target = (window(w_out, i), m_out.at[i], v_out.at[i])[k]
        return pltpu.make_async_copy(parts[k][1].at[i], target, store_sem.at[k, i])

    def fetch(i, n, side):
        return pltpu.make_async_copy(
            x_refs[n * sides + side].at[:, pl.ds(pl.multiple_of(lane[i] * TILE, TILE), TILE)],
            x_buf.at[i, pl.ds(side * rows, rows), :],
            x_sem.at[side, i],
        )

    @pl.loop(0, slots)
    def _(i):
        @pl.when(owned[i] > 0)
        def _():
            for n in range(count):

                @pl.when(piece[i] == n)
                def _():
                    for side in range(sides):
                        fetch(i, n, side).start()

            for k in range(3):
                load(i, k).start()

    @pl.loop(0, slots)
    def _(i):
        @pl.when(owned[i] > 0)
        def _():
            for side in range(sides):
                fetch(i, 0, side).wait()
            cot = cot_ref[:, pl.ds(pl.multiple_of(i // CAP * TILE, TILE), TILE)]
            gradient = lax.dot_general(
                x_buf[i], cot, (((0,), (0,)), ((), ())), preferred_element_type=jnp.float32
            )
            for k in range(3):
                load(i, k).wait()
            m = beta_one * m_buf[i] + (1.0 - beta_one) * gradient
            v = beta_two * v_buf[i] + (1.0 - beta_two) * gradient * gradient
            step = m / bias_one / (jnp.sqrt(v / bias_two) + eps_adam)
            w = w_buf[i] - learn_rate * step
            w_buf[i], m_buf[i], v_buf[i] = w, m, v
            fresh_ref[i] = w.astype(jnp.bfloat16)
            for k in range(3):
                store(i, k).start()

        @pl.when(owned[i] == 0)
        def _():
            fresh_ref[i] = jnp.zeros((TILE, TILE), jnp.bfloat16)

    @pl.loop(0, slots)
    def _(i):
        @pl.when(owned[i] > 0)
        def _():
            for k in range(3):
                store(i, k).wait()


def update_tiles(owned, row, piece, lane, x_parts, count, cot, w, m, v):
    slots = owned.shape[0]
    sides = len(x_parts) // count
    smem = pl.BlockSpec(memory_space=pltpu.SMEM)
    vmem = pl.BlockSpec(memory_space=pltpu.VMEM)
    hbm = pl.BlockSpec(memory_space=pl.ANY)
    state = jax.ShapeDtypeStruct((slots, TILE, TILE), jnp.float32)
    buf = pltpu.VMEM((slots, TILE, TILE), jnp.float32)
    sems = pltpu.SemaphoreType.DMA((3, slots))
    return pl.pallas_call(
        functools.partial(tile_kernel, slots, count, sides),
        out_shape=(
            jax.ShapeDtypeStruct(w.shape, w.dtype),
            state,
            state,
            jax.ShapeDtypeStruct(state.shape, jnp.bfloat16),
        ),
        in_specs=[smem] * 4 + [vmem] * (len(x_parts) + 1) + [hbm] * 3,
        out_specs=(hbm, hbm, hbm, vmem),
        scratch_shapes=[buf, buf, buf, pltpu.VMEM((slots, cot.shape[0], TILE), jnp.bfloat16)]
        + [sems, pltpu.SemaphoreType.DMA((sides, slots)), sems],
        input_output_aliases={5 + len(x_parts): 0},
        cost_estimate=pl.CostEstimate(
            flops=2 * slots * TILE * TILE * cot.shape[0],
            bytes_accessed=26 * slots * TILE * TILE,
            transcendentals=slots * TILE * TILE,
        ),
        name="update_tiles",
    )(owned, row, piece, lane, *x_parts, cot, w, m, v)


CHUNKS = 8
DEPTH = 8


def finish_steps(slots, owned, row, a_ref, new_ref, out_ref, ring, tiles, sems, work):
    in_sem, out_sem, tile_sem = sems
    height = ring.shape[1]

    def load(c):
        source = a_ref.at[pl.ds(c * height, height), :]
        return pltpu.make_async_copy(source, ring.at[c % DEPTH], in_sem.at[c % DEPTH])

    def store(c):
        target = out_ref.at[pl.ds(c * height, height), :]
        return pltpu.make_async_copy(ring.at[c % DEPTH], target, out_sem.at[c % DEPTH])

    def fetch(i):
        return pltpu.make_async_copy(new_ref.at[i], tiles.at[i], tile_sem.at[i])

    def put(i):
        target = out_ref.at[
            pl.ds(pl.multiple_of(row[i] * TILE, TILE), TILE),
            pl.ds(pl.multiple_of(i // CAP * TILE, TILE), TILE),
        ]
        return pltpu.make_async_copy(tiles.at[i], target, tile_sem.at[i])

    def each(do):
        @pl.loop(0, slots)
        def _(i):
            @pl.when(owned[i] > 0)
            def _():
                do(i)

    for c in range(min(DEPTH, CHUNKS)):
        load(c).start()
    each(lambda i: fetch(i).start())
    waited = 0
    for c in range(CHUNKS):
        if c >= 2 and c - 2 + DEPTH < CHUNKS:
            store(c - 2).wait()
            waited = c - 1
            load(c - 2 + DEPTH).start()
        load(c).wait()
        store(c).start()
        if c < len(work):
            work[c]()
    each(lambda i: fetch(i).wait())
    for c in range(waited, CHUNKS):
        store(c).wait()
    each(lambda i: put(i).start())
    for step in work[CHUNKS:]:
        step()
    each(lambda i: put(i).wait())


def product_steps(count, x_refs, w_ref, base_ref, sum_ref):
    rows = x_refs[0].shape[0]

    def step(k):
        n, side = divmod(k, 2)
        into = pl.ds(side * rows, rows)
        product = jnp.dot(x_refs[k][...], w_ref[n], preferred_element_type=jnp.float32)
        if n > 0:
            sum_ref[into, :] += product
        elif base_ref is not None:
            sum_ref[into, :] = base_ref[into, :] + product
        else:
            sum_ref[into, :] = product

    return [functools.partial(step, k) for k in range(2 * count)]


def low_kernel(slots, count, owned, row, *refs):
    w_ref, a_ref, new_ref, sum_ref, out_ref, ring, tiles, *sems = refs[2 * count :]
    work = product_steps(count, refs[: 2 * count], w_ref, None, sum_ref)
    finish_steps(slots, owned, row, a_ref, new_ref, out_ref, ring, tiles, sems, work)


def turned_kernel(count, *refs):
    w_ref, base_ref, turn_ref, mine_ref, give_ref, sum_ref = refs[2 * count :]
    for step in product_steps(count, refs[: 2 * count], w_ref, base_ref, sum_ref):
        step()
    total, rows = sum_ref.shape[0], mine_ref.shape[0]
    place = lax.broadcasted_iota(jnp.int32, (total, rows), 0)

    def rows_of(side, values):
        chosen = place == turn_ref[:, side * rows : (side + 1) * rows]
        return lax.dot_general(
            chosen.astype(jnp.bfloat16), values, (((0,), (0,)), ((), ())),
            preferred_element_type=jnp.float32,
        )

    value = sum_ref[...]
    head = value.astype(jnp.bfloat16)
    rest = (value - head.astype(jnp.float32)).astype(jnp.bfloat16)
    give_ref[...] = rows_of(1, head).astype(jnp.bfloat16)
    mine_ref[...] = rows_of(0, head) + rows_of(0, rest)


def turned_product(parts, half, base, turn):
    count = half.shape[0]
    rows, depth = parts[0].shape
    width = half.shape[2]
    vmem = pl.BlockSpec(memory_space=pltpu.VMEM)
    return pl.pallas_call(
        functools.partial(turned_kernel, count),
        out_shape=(
            jax.ShapeDtypeStruct((rows, width), jnp.float32),
            jax.ShapeDtypeStruct((rows, width), jnp.bfloat16),
        ),
        in_specs=[vmem] * (2 * count + 3),
        out_specs=(vmem, vmem),
        scratch_shapes=[pltpu.VMEM((2 * rows, width), jnp.float32)],
        cost_estimate=pl.CostEstimate(
            flops=4 * count * rows * width * depth,
            bytes_accessed=2 * count * depth * (2 * rows + width),
            transcendentals=0,
        ),
        name="turned_product",
    )(*parts, half, base, turn)


def plain_kernel(slots, owned, row, a_ref, new_ref, out_ref, ring, tiles, *sems):
    finish_steps(slots, owned, row, a_ref, new_ref, out_ref, ring, tiles, sems, [])


def finish_state(owned, row, a, new, parts=(), half=None):
    slots = owned.shape[0]
    count = len(parts) // 2
    smem = pl.BlockSpec(memory_space=pltpu.SMEM)
    vmem = pl.BlockSpec(memory_space=pltpu.VMEM)
    hbm = pl.BlockSpec(memory_space=pl.ANY)
    outs, operands, scratch = [], list(parts), []
    kernel = functools.partial(plain_kernel, slots)
    if parts:
        operands.append(half)
        kernel = functools.partial(low_kernel, slots, count)
        outs = [jax.ShapeDtypeStruct((2 * parts[0].shape[0], half.shape[2]), jnp.float32)]
    scratch += [
        pltpu.VMEM((DEPTH, a.shape[0] // CHUNKS, a.shape[1]), a.dtype),
        pltpu.VMEM((slots, TILE, TILE), a.dtype),
        pltpu.SemaphoreType.DMA((DEPTH,)),
        pltpu.SemaphoreType.DMA((DEPTH,)),
        pltpu.SemaphoreType.DMA((slots,)),
    ]
    flops = sum(2 * p.size * half.shape[2] for p in parts)
    return pl.pallas_call(
        kernel,
        out_shape=outs + [jax.ShapeDtypeStruct(a.shape, a.dtype)],
        in_specs=[smem, smem] + [vmem] * len(operands) + [hbm, hbm],
        out_specs=[vmem] * len(outs) + [hbm],
        scratch_shapes=scratch,
        cost_estimate=pl.CostEstimate(
            flops=flops, bytes_accessed=8 * a.size, transcendentals=0
        ),
        name="finish_state",
    )(owned, row, *operands, a, new)


def swap(a, axis, size, bit):
    return lax.ppermute(a, axis, [(i, i ^ bit) for i in range(size)])


def owned_slots(tile_mask, group_at, shard_at, row_tiles, col_tiles):
    mask_cols = lax.dynamic_slice_in_dim(tile_mask, shard_at * col_tiles, col_tiles, 1)
    count = tile_mask.shape[0]
    at = jnp.arange(count)
    before = (at[None, :] < at[:, None]).astype(jnp.float32)
    rank = jnp.dot(before, mask_cols.astype(jnp.float32)).astype(jnp.int32)
    hit = (mask_cols[:, :, None] > 0) & (rank[:, :, None] == jnp.arange(CAP)[None, None, :])
    row = jnp.sum(jnp.where(hit, at[:, None, None], 0), axis=0).reshape(-1)
    live = jnp.sum(hit.astype(jnp.int32), axis=0).reshape(-1)
    owned = jnp.where(row // row_tiles == group_at, live, 0)
    return owned, row - group_at * row_tiles


def pair_shards(groups, shard_count, rollout_rows, assign, cotangent, w_master, adam_m, adam_v, tile_mask):
    group_at = lax.axis_index("group")
    shard_at = lax.axis_index("shard")
    row_count, features = rollout_rows.shape
    width = cotangent.shape[1]
    col_tiles = width // TILE
    row_tiles = w_master.shape[0] // TILE
    half_count = shard_count // 2
    bits = [half_count >> (k + 1) for k in range(half_count.bit_length() - 1)]
    offsets = [0]
    for bit in bits:
        offsets = offsets + [o | bit for o in offsets]
    base = shard_at % half_count
    order = base ^ jnp.asarray(offsets, jnp.int32)
    in_half = shard_at // half_count == group_at

    blocks = w_master.reshape(half_count, features, width)
    low = half_count // 2

    row_total = groups * row_count
    start = group_at * row_count
    turned = jnp.where(group_at == 0, assign, jnp.concatenate([assign[row_count:], assign[:row_count]]))
    turned = jnp.where(turned >= start, turned - start, turned + row_total - start)

    owned, row = owned_slots(tile_mask, group_at, shard_at, row_tiles, col_tiles)
    per_block = features // TILE
    block = jnp.clip(row // per_block, 0, half_count - 1) ^ base
    piece = sum(jnp.where(block & bit > 0, 1 << k, 0) for k, bit in enumerate(bits))
    lane = lax.rem(row + row_tiles * groups, per_block)
    piece = piece.astype(jnp.int32)
    turn = turned.reshape(1, row_total)

    cot_other = swap(cotangent, "group", groups, 1)
    far = swap(rollout_rows, "shard", shard_count, half_count)
    w_copy, half_high = cast_pass(blocks, order, low, (owned, row, piece, lane, turn))
    sent = back_product(cotangent, cot_other, half_high)
    got = swap(sent, "shard", shard_count, bits[-1])
    keep = jnp.where(in_half, rollout_rows, far)
    give = jnp.where(in_half, far, rollout_rows)
    x_parts = [keep, swap(give, "group", groups, 1)]
    for bit in bits:
        held = list(x_parts)
        for part in held:
            x_parts.append(swap(part, "shard", shard_count, bit))

    w_copy, half_low, kept = weight_pass(cotangent, cot_other, blocks, order, low, w_copy)
    cot_turned = turn_rows(cotangent, cot_other, turn)
    terms = {
        o: kept[n].astype(jnp.float32) + got[n].astype(jnp.float32)
        for n, o in enumerate(offsets[:low])
    }
    for bit in bits[:-1]:
        for o in sorted([o for o in terms if o & bit], reverse=True):
            term = swap(terms.pop(o).astype(jnp.bfloat16), "shard", shard_count, bit)
            terms[o ^ bit] = terms[o ^ bit] + term.astype(jnp.float32)
    done = terms[0].reshape(groups, row_count, features)
    other = swap(done[1].astype(jnp.bfloat16), "group", groups, 1).astype(jnp.float32)
    near = jnp.where(in_half, done[0], other)
    away = jnp.where(in_half, other, done[0]).astype(jnp.bfloat16)
    back = swap(away, "shard", shard_count, half_count).astype(jnp.float32)
    input_grad = (near + back).astype(jnp.bfloat16)

    w_updated, m_new, v_new, fresh = update_tiles(
        owned, row, piece, lane, x_parts, half_count, cot_turned,
        w_copy.reshape(w_master.shape), adam_m, adam_v,
    )
    tiles = fresh + swap(fresh, "group", groups, 1)
    rollout_tiles = tiles.reshape(col_tiles, CAP, TILE, TILE)

    partial, m_updated = finish_state(
        owned, row, adam_m, m_new, x_parts[: 2 * low], half_low
    )
    mine, give = turned_product(x_parts[2 * low :], half_high, partial, turn)
    (v_updated,) = finish_state(owned, row, adam_v, v_new)
    taken = swap(give, "group", groups, 1).astype(jnp.float32)
    projected = (mine + taken).astype(jnp.bfloat16)
    return (projected, input_grad, w_updated, m_updated, v_updated, rollout_tiles)


def any_shards(groups, shard_count, rollout_rows, assign, cotangent, w_master, adam_m, adam_v, tile_mask):
    group_at = lax.axis_index("group")
    shard_at = lax.axis_index("shard")
    row_count, features = rollout_rows.shape
    width = cotangent.shape[1]
    col_tiles = width // TILE
    row_tiles = w_master.shape[0] // TILE
    per_group = shard_count // groups
    row_total = groups * row_count
    order = jnp.arange(per_group, dtype=jnp.int32)
    w_copy, half = cast_pass(w_master.reshape(per_group, -1, width), order)
    x_cols = lax.all_gather(rollout_rows, "group", axis=0, tiled=True)
    x_full = lax.all_gather(x_cols, "shard", axis=0)
    x_all = lax.dynamic_slice_in_dim(x_full, group_at * per_group, per_group, 0)
    cot_all = lax.all_gather(cotangent, "group", axis=0, tiled=True)
    middle = row_total // 2
    products = back_product(cot_all[:middle], cot_all[middle:], half)
    products = products.reshape(per_group, groups, row_count, features)
    products = products.transpose(1, 0, 2, 3).reshape(shard_count * row_count, features)
    summed = lax.psum_scatter(products, "shard", scatter_dimension=0, tiled=True)
    moves = [
        (g * shard_count + r * per_group + k, r * shard_count + g * per_group + k)
        for g in range(groups)
        for r in range(groups)
        for k in range(per_group)
    ]
    input_grad = lax.ppermute(summed, ("group", "shard"), moves)
    pick = (jnp.arange(row_total)[:, None] == assign[None, :]).astype(jnp.bfloat16)
    cot_turned = jnp.dot(pick, cot_all, preferred_element_type=jnp.float32).astype(jnp.bfloat16)
    partial = jnp.take(forward_product(x_all, half), assign, axis=0)
    projected = lax.psum_scatter(partial, "group", scatter_dimension=0, tiled=True)
    projected = projected.astype(jnp.bfloat16)
    owned, row = owned_slots(tile_mask, group_at, shard_at, row_tiles, col_tiles)
    per_block = features // TILE
    piece = jnp.clip(row // per_block, 0, per_group - 1)
    lane = lax.rem(row + row_tiles * groups, per_block)
    w_updated, m_new, v_new, fresh = update_tiles(
        owned, row, piece, lane, list(x_all), per_group, cot_turned,
        w_copy.reshape(w_master.shape), adam_m, adam_v,
    )
    (m_updated,) = finish_state(owned, row, adam_m, m_new)
    (v_updated,) = finish_state(owned, row, adam_v, v_new)
    rollout_tiles = lax.psum(fresh, "group").reshape(col_tiles, CAP, TILE, TILE)
    return (projected, input_grad, w_updated, m_updated, v_updated, rollout_tiles)


def solution(mesh):
    groups, shard_count = mesh.shape["group"], mesh.shape["shard"]
    paired = groups == 2 and shard_count == 16
    inner = functools.partial(pair_shards if paired else any_shards, groups, shard_count)

    placed = (
        P("group", "shard"),
        P(),
        P("group", "shard"),
        P("group", "shard"),
        P("group", "shard"),
        P("group", "shard"),
        P(),
    )
    return jax.shard_map(
        inner,
        mesh=mesh,
        in_specs=placed,
        out_specs=(
            P("group", "shard"),
            P("group", "shard"),
            P("group", "shard"),
            P("group", "shard"),
            P("group", "shard"),
            P("shard", None, None, None),
        ),
        check_vma=False,
    )
```

```python
import functools

import jax
import jax.numpy as jnp
from jax import lax
from jax.experimental import pallas as pl
from jax.experimental.pallas import tpu as pltpu
from jax.sharding import PartitionSpec as P


TILE = 128
CAP = 6


beta_one = 0.9
beta_two = 0.999
learn_rate = 0.02
eps_adam = 1e-08
bias_one = 1.0 - 0.9**10
bias_two = 1.0 - 0.999**10


def cast_kernel(order, w_ref, *refs):
    copy_ref, half_ref = refs[-2:]
    w = w_ref[...]
    copy_ref[...] = w
    half_ref[...] = w.astype(jnp.bfloat16)


def cast_pass(blocks, order, first=0, after=()):
    count = order.shape[0] - first
    _, depth, width = blocks.shape
    take = pl.BlockSpec((1, depth, width), lambda i, order: (order[i + first], 0, 0))
    put = pl.BlockSpec((1, depth, width), lambda i, order: (i, 0, 0))
    return pl.pallas_call(
        cast_kernel,
        out_shape=(
            jax.ShapeDtypeStruct(blocks.shape, jnp.float32),
            jax.ShapeDtypeStruct((count, depth, width), jnp.bfloat16),
        ),
        grid_spec=pltpu.PrefetchScalarGridSpec(
            num_scalar_prefetch=1,
            grid=(count,),
            in_specs=[take] + [pl.BlockSpec(memory_space=pl.ANY)] * len(after),
            out_specs=(take, put),
        ),
        cost_estimate=pl.CostEstimate(
            flops=0, bytes_accessed=10 * count * depth * width, transcendentals=0
        ),
        name="cast_pass",
    )(order, blocks, *after)


def back_kernel(near_ref, other_ref, half_ref, out_ref, cot_ref):
    rows = near_ref.shape[0]

    @pl.when(pl.program_id(0) == 0)
    def _():
        cot_ref[:rows, :] = near_ref[...]
        cot_ref[rows:, :] = other_ref[...]

    out_ref[0] = lax.dot_general(
        cot_ref[...], half_ref[0], (((1,), (1,)), ((), ())), preferred_element_type=jnp.float32
    ).astype(out_ref.dtype)


def back_product(near, other, half):
    count, depth, width = half.shape
    rows = near.shape[0] + other.shape[0]
    vmem = pl.BlockSpec(memory_space=pltpu.VMEM)
    return pl.pallas_call(
        back_kernel,
        out_shape=jax.ShapeDtypeStruct((count, rows, depth), jnp.bfloat16),
        grid=(count,),
        in_specs=[vmem, vmem, pl.BlockSpec((1, depth, width), lambda i: (i, 0, 0))],
        out_specs=pl.BlockSpec((1, rows, depth), lambda i: (i, 0, 0)),
        scratch_shapes=[pltpu.VMEM((rows, width), jnp.bfloat16)],
        cost_estimate=pl.CostEstimate(
            flops=2 * count * rows * width * depth,
            bytes_accessed=2 * count * depth * (width + rows),
            transcendentals=0,
        ),
        name="back_product",
    )(near, other, half)


def weight_kernel(
    order, near_ref, other_ref, w_ref, _, copy_ref, half_ref, out_ref, cot_ref
):
    rows = near_ref.shape[0]

    @pl.when(pl.program_id(0) == 0)
    def _():
        cot_ref[:rows, :] = near_ref[...]
        cot_ref[rows:, :] = other_ref[...]

    w = w_ref[0]
    copy_ref[0] = w
    half = w.astype(jnp.bfloat16)
    half_ref[0] = half
    out_ref[0] = lax.dot_general(
        cot_ref[...], half, (((1,), (1,)), ((), ())), preferred_element_type=jnp.float32
    ).astype(out_ref.dtype)


def turn_kernel(near_ref, other_ref, turn_ref, out_ref):
    rows = near_ref.shape[0]
    place = lax.broadcasted_iota(jnp.int32, (2 * rows, 2 * rows), 0)
    chosen = (place == turn_ref[...]).astype(jnp.bfloat16)
    cot = jnp.concatenate([near_ref[...], other_ref[...]], axis=0)
    out_ref[...] = jnp.dot(chosen, cot, preferred_element_type=jnp.float32).astype(jnp.bfloat16)


def turn_rows(near, other, turn):
    rows, width = near.shape
    vmem = pl.BlockSpec(memory_space=pltpu.VMEM)
    return pl.pallas_call(
        turn_kernel,
        out_shape=jax.ShapeDtypeStruct((2 * rows, width), jnp.bfloat16),
        in_specs=[vmem] * 3,
        out_specs=vmem,
        cost_estimate=pl.CostEstimate(
            flops=8 * rows * rows * width, bytes_accessed=8 * rows * width, transcendentals=0
        ),
        name="turn_rows",
    )(near, other, turn)


def weight_pass(near, other, blocks, order, count, copied):
    width = near.shape[1]
    rows = near.shape[0] + other.shape[0]
    depth = blocks.shape[1]
    vmem = pl.BlockSpec(memory_space=pltpu.VMEM)
    take = pl.BlockSpec((1, depth, width), lambda i, order: (order[i], 0, 0))
    put = pl.BlockSpec((1, depth, width), lambda i, order: (i, 0, 0))
    out = pl.BlockSpec((1, rows, depth), lambda i, order: (i, 0, 0))
    return pl.pallas_call(
        weight_kernel,
        out_shape=(
            jax.ShapeDtypeStruct(blocks.shape, jnp.float32),
            jax.ShapeDtypeStruct((count, depth, width), jnp.bfloat16),
            jax.ShapeDtypeStruct((count, rows, depth), jnp.bfloat16),
        ),
        grid_spec=pltpu.PrefetchScalarGridSpec(
            num_scalar_prefetch=1,
            grid=(count,),
            in_specs=[vmem, vmem, take, pl.BlockSpec(memory_space=pl.ANY)],
            out_specs=(take, put, out),
            scratch_shapes=[pltpu.VMEM((rows, width), jnp.bfloat16)],
        ),
        input_output_aliases={4: 0},
        cost_estimate=pl.CostEstimate(
            flops=2 * count * rows * width * depth,
            bytes_accessed=count * depth * (10 * width + 2 * rows),
            transcendentals=0,
        ),
        name="weight_pass",
    )(order, near, other, blocks, copied)


def forward_kernel(x_ref, w_ref, out_ref):
    product = jnp.dot(x_ref[0], w_ref[0], preferred_element_type=jnp.float32)

    @pl.when(pl.program_id(0) == 0)
    def _():
        out_ref[...] = product

    @pl.when(pl.program_id(0) > 0)
    def _():
        out_ref[...] += product


def forward_product(x, half):
    count, rows, depth = x.shape
    width = half.shape[2]
    return pl.pallas_call(
        forward_kernel,
        out_shape=jax.ShapeDtypeStruct((rows, width), jnp.float32),
        grid=(count,),
        in_specs=[
            pl.BlockSpec((1, rows, depth), lambda i: (i, 0, 0)),
            pl.BlockSpec((1, depth, width), lambda i: (i, 0, 0)),
        ],
        out_specs=pl.BlockSpec((rows, width), lambda i: (0, 0)),
        cost_estimate=pl.CostEstimate(
            flops=2 * count * rows * width * depth,
            bytes_accessed=2 * count * depth * (rows + width),
            transcendentals=0,
        ),
        name="forward_product",
    )(x, half)


def tile_kernel(slots, count, sides, owned, row, piece, lane, *refs):
    x_refs = refs[: count * sides]
    (
        cot_ref, w_in, m_in, v_in, w_out, m_out, v_out, fresh_ref,
        w_buf, m_buf, v_buf, x_buf, load_sem, store_sem,
    ) = refs[count * sides :]
    parts = ((w_in, w_buf), (m_in, m_buf), (v_in, v_buf))
    rows = x_refs[0].shape[0]

    def window(ref, i):
        return ref.at[
            pl.ds(pl.multiple_of(row[i] * TILE, TILE), TILE),
            pl.ds(pl.multiple_of(i // CAP * TILE, TILE), TILE),
        ]

    def load(i, k):
        source, buf = parts[k]
        return pltpu.make_async_copy(window(source, i), buf.at[i], load_sem.at[k, i])

    def store(i, k):
        target = (window(w_out, i), m_out.at[i], v_out.at[i])[k]
        return pltpu.make_async_copy(parts[k][1].at[i], target, store_sem.at[k, i])

    @pl.loop(0, slots)
    def _(i):
        @pl.when(owned[i] > 0)
        def _():
            for k in range(3):
                load(i, k).start()

    @pl.loop(0, slots)
    def _(i):
        @pl.when(owned[i] > 0)
        def _():
            columns = pl.ds(pl.multiple_of(lane[i] * TILE, TILE), TILE)
            for n in range(count):

                @pl.when(piece[i] == n)
                def _():
                    for side in range(sides):
                        x_buf[side * rows : (side + 1) * rows, :] = x_refs[n * sides + side][
                            :, columns
                        ]

            cot = cot_ref[:, pl.ds(pl.multiple_of(i // CAP * TILE, TILE), TILE)]
            gradient = lax.dot_general(
                x_buf[...], cot, (((0,), (0,)), ((), ())), preferred_element_type=jnp.float32
            )
            for k in range(3):
                load(i, k).wait()
            m = beta_one * m_buf[i] + (1.0 - beta_one) * gradient
            v = beta_two * v_buf[i] + (1.0 - beta_two) * gradient * gradient
            step = m / bias_one / (jnp.sqrt(v / bias_two) + eps_adam)
            w = w_buf[i] - learn_rate * step
            w_buf[i], m_buf[i], v_buf[i] = w, m, v
            fresh_ref[i] = w.astype(jnp.bfloat16)
            for k in range(3):
                store(i, k).start()

        @pl.when(owned[i] == 0)
        def _():
            fresh_ref[i] = jnp.zeros((TILE, TILE), jnp.bfloat16)

    @pl.loop(0, slots)
    def _(i):
        @pl.when(owned[i] > 0)
        def _():
            for k in range(3):
                store(i, k).wait()


def update_tiles(owned, row, piece, lane, x_parts, count, cot, w, m, v):
    slots = owned.shape[0]
    sides = len(x_parts) // count
    smem = pl.BlockSpec(memory_space=pltpu.SMEM)
    vmem = pl.BlockSpec(memory_space=pltpu.VMEM)
    hbm = pl.BlockSpec(memory_space=pl.ANY)
    state = jax.ShapeDtypeStruct((slots, TILE, TILE), jnp.float32)
    buf = pltpu.VMEM((slots, TILE, TILE), jnp.float32)
    sems = pltpu.SemaphoreType.DMA((3, slots))
    return pl.pallas_call(
        functools.partial(tile_kernel, slots, count, sides),
        out_shape=(
            jax.ShapeDtypeStruct(w.shape, w.dtype),
            state,
            state,
            jax.ShapeDtypeStruct(state.shape, jnp.bfloat16),
        ),
        in_specs=[smem] * 4 + [vmem] * (len(x_parts) + 1) + [hbm] * 3,
        out_specs=(hbm, hbm, hbm, vmem),
        scratch_shapes=[buf, buf, buf, pltpu.VMEM((cot.shape[0], TILE), jnp.bfloat16)]
        + [sems, sems],
        input_output_aliases={5 + len(x_parts): 0},
        cost_estimate=pl.CostEstimate(
            flops=2 * slots * TILE * TILE * cot.shape[0],
            bytes_accessed=26 * slots * TILE * TILE,
            transcendentals=slots * TILE * TILE,
        ),
        name="update_tiles",
    )(owned, row, piece, lane, *x_parts, cot, w, m, v)


CHUNKS = 8
DEPTH = 8


def finish_steps(slots, owned, row, a_ref, new_ref, out_ref, ring, tiles, sems, work):
    in_sem, out_sem, tile_sem = sems
    height = ring.shape[1]

    def load(c):
        source = a_ref.at[pl.ds(c * height, height), :]
        return pltpu.make_async_copy(source, ring.at[c % DEPTH], in_sem.at[c % DEPTH])

    def store(c):
        target = out_ref.at[pl.ds(c * height, height), :]
        return pltpu.make_async_copy(ring.at[c % DEPTH], target, out_sem.at[c % DEPTH])

    def fetch(i):
        return pltpu.make_async_copy(new_ref.at[i], tiles.at[i], tile_sem.at[i])

    def put(i):
        target = out_ref.at[
            pl.ds(pl.multiple_of(row[i] * TILE, TILE), TILE),
            pl.ds(pl.multiple_of(i // CAP * TILE, TILE), TILE),
        ]
        return pltpu.make_async_copy(tiles.at[i], target, tile_sem.at[i])

    def each(do):
        @pl.loop(0, slots)
        def _(i):
            @pl.when(owned[i] > 0)
            def _():
                do(i)

    for c in range(min(DEPTH, CHUNKS)):
        load(c).start()
    each(lambda i: fetch(i).start())
    waited = 0
    for c in range(CHUNKS):
        if c >= 2 and c - 2 + DEPTH < CHUNKS:
            store(c - 2).wait()
            waited = c - 1
            load(c - 2 + DEPTH).start()
        load(c).wait()
        store(c).start()
        if c < len(work):
            work[c]()
    each(lambda i: fetch(i).wait())
    for c in range(waited, CHUNKS):
        store(c).wait()
    each(lambda i: put(i).start())
    for step in work[CHUNKS:]:
        step()
    each(lambda i: put(i).wait())


def product_steps(count, x_refs, w_ref, base_ref, sum_ref):
    rows = x_refs[0].shape[0]

    def step(k):
        n, side = divmod(k, 2)
        into = pl.ds(side * rows, rows)
        product = jnp.dot(x_refs[k][...], w_ref[n], preferred_element_type=jnp.float32)
        if n > 0:
            sum_ref[into, :] += product
        elif base_ref is not None:
            sum_ref[into, :] = base_ref[into, :] + product
        else:
            sum_ref[into, :] = product

    return [functools.partial(step, k) for k in range(2 * count)]


def low_kernel(slots, count, owned, row, *refs):
    w_ref, a_ref, new_ref, sum_ref, out_ref, ring, tiles, *sems = refs[2 * count :]
    work = product_steps(count, refs[: 2 * count], w_ref, None, sum_ref)
    finish_steps(slots, owned, row, a_ref, new_ref, out_ref, ring, tiles, sems, work)


def turned_kernel(count, *refs):
    w_ref, base_ref, turn_ref, mine_ref, give_ref, sum_ref = refs[2 * count :]
    for step in product_steps(count, refs[: 2 * count], w_ref, base_ref, sum_ref):
        step()
    total, rows = sum_ref.shape[0], mine_ref.shape[0]
    place = lax.broadcasted_iota(jnp.int32, (total, rows), 0)

    def rows_of(side, values):
        chosen = place == turn_ref[:, side * rows : (side + 1) * rows]
        return lax.dot_general(
            chosen.astype(jnp.bfloat16), values, (((0,), (0,)), ((), ())),
            preferred_element_type=jnp.float32,
        )

    value = sum_ref[...]
    head = value.astype(jnp.bfloat16)
    rest = (value - head.astype(jnp.float32)).astype(jnp.bfloat16)
    give_ref[...] = rows_of(1, head).astype(jnp.bfloat16)
    mine_ref[...] = rows_of(0, head) + rows_of(0, rest)


def turned_product(parts, half, base, turn):
    count = half.shape[0]
    rows, depth = parts[0].shape
    width = half.shape[2]
    vmem = pl.BlockSpec(memory_space=pltpu.VMEM)
    return pl.pallas_call(
        functools.partial(turned_kernel, count),
        out_shape=(
            jax.ShapeDtypeStruct((rows, width), jnp.float32),
            jax.ShapeDtypeStruct((rows, width), jnp.bfloat16),
        ),
        in_specs=[vmem] * (2 * count + 3),
        out_specs=(vmem, vmem),
        scratch_shapes=[pltpu.VMEM((2 * rows, width), jnp.float32)],
        cost_estimate=pl.CostEstimate(
            flops=4 * count * rows * width * depth,
            bytes_accessed=2 * count * depth * (2 * rows + width),
            transcendentals=0,
        ),
        name="turned_product",
    )(*parts, half, base, turn)


def plain_kernel(slots, owned, row, a_ref, new_ref, out_ref, ring, tiles, *sems):
    finish_steps(slots, owned, row, a_ref, new_ref, out_ref, ring, tiles, sems, [])


def finish_state(owned, row, a, new, parts=(), half=None):
    slots = owned.shape[0]
    count = len(parts) // 2
    smem = pl.BlockSpec(memory_space=pltpu.SMEM)
    vmem = pl.BlockSpec(memory_space=pltpu.VMEM)
    hbm = pl.BlockSpec(memory_space=pl.ANY)
    outs, operands, scratch = [], list(parts), []
    kernel = functools.partial(plain_kernel, slots)
    if parts:
        operands.append(half)
        kernel = functools.partial(low_kernel, slots, count)
        outs = [jax.ShapeDtypeStruct((2 * parts[0].shape[0], half.shape[2]), jnp.float32)]
    scratch += [
        pltpu.VMEM((DEPTH, a.shape[0] // CHUNKS, a.shape[1]), a.dtype),
        pltpu.VMEM((slots, TILE, TILE), a.dtype),
        pltpu.SemaphoreType.DMA((DEPTH,)),
        pltpu.SemaphoreType.DMA((DEPTH,)),
        pltpu.SemaphoreType.DMA((slots,)),
    ]
    flops = sum(2 * p.size * half.shape[2] for p in parts)
    return pl.pallas_call(
        kernel,
        out_shape=outs + [jax.ShapeDtypeStruct(a.shape, a.dtype)],
        in_specs=[smem, smem] + [vmem] * len(operands) + [hbm, hbm],
        out_specs=[vmem] * len(outs) + [hbm],
        scratch_shapes=scratch,
        cost_estimate=pl.CostEstimate(
            flops=flops, bytes_accessed=8 * a.size, transcendentals=0
        ),
        name="finish_state",
    )(owned, row, *operands, a, new)


def swap(a, axis, size, bit):
    return lax.ppermute(a, axis, [(i, i ^ bit) for i in range(size)])


def owned_slots(tile_mask, group_at, shard_at, row_tiles, col_tiles):
    mask_cols = lax.dynamic_slice_in_dim(tile_mask, shard_at * col_tiles, col_tiles, 1)
    count = tile_mask.shape[0]
    at = jnp.arange(count)
    before = (at[None, :] < at[:, None]).astype(jnp.float32)
    rank = jnp.dot(before, mask_cols.astype(jnp.float32)).astype(jnp.int32)
    hit = (mask_cols[:, :, None] > 0) & (rank[:, :, None] == jnp.arange(CAP)[None, None, :])
    row = jnp.sum(jnp.where(hit, at[:, None, None], 0), axis=0).reshape(-1)
    live = jnp.sum(hit.astype(jnp.int32), axis=0).reshape(-1)
    owned = jnp.where(row // row_tiles == group_at, live, 0)
    return owned, row - group_at * row_tiles


def pair_shards(groups, shard_count, rollout_rows, assign, cotangent, w_master, adam_m, adam_v, tile_mask):
    group_at = lax.axis_index("group")
    shard_at = lax.axis_index("shard")
    row_count, features = rollout_rows.shape
    width = cotangent.shape[1]
    col_tiles = width // TILE
    row_tiles = w_master.shape[0] // TILE
    half_count = shard_count // 2
    bits = [half_count >> (k + 1) for k in range(half_count.bit_length() - 1)]
    offsets = [0]
    for bit in bits:
        offsets = offsets + [o | bit for o in offsets]
    base = shard_at % half_count
    order = base ^ jnp.asarray(offsets, jnp.int32)
    in_half = shard_at // half_count == group_at

    blocks = w_master.reshape(half_count, features, width)
    low = half_count // 2

    row_total = groups * row_count
    start = group_at * row_count
    turned = jnp.where(group_at == 0, assign, jnp.concatenate([assign[row_count:], assign[:row_count]]))
    turned = jnp.where(turned >= start, turned - start, turned + row_total - start)

    owned, row = owned_slots(tile_mask, group_at, shard_at, row_tiles, col_tiles)
    per_block = features // TILE
    block = jnp.clip(row // per_block, 0, half_count - 1) ^ base
    piece = sum(jnp.where(block & bit > 0, 1 << k, 0) for k, bit in enumerate(bits))
    lane = lax.rem(row + row_tiles * groups, per_block)
    piece = piece.astype(jnp.int32)
    turn = turned.reshape(1, row_total)

    cot_other = swap(cotangent, "group", groups, 1)
    far = swap(rollout_rows, "shard", shard_count, half_count)
    w_copy, half_high = cast_pass(blocks, order, low, (owned, row, piece, lane, turn))
    sent = back_product(cotangent, cot_other, half_high)
    got = swap(sent, "shard", shard_count, bits[-1])
    keep = jnp.where(in_half, rollout_rows, far)
    give = jnp.where(in_half, far, rollout_rows)
    x_parts = [keep, swap(give, "group", groups, 1)]
    for bit in bits:
        held = list(x_parts)
        for part in held:
            x_parts.append(swap(part, "shard", shard_count, bit))

    w_copy, half_low, kept = weight_pass(cotangent, cot_other, blocks, order, low, w_copy)
    cot_turned = turn_rows(cotangent, cot_other, turn)
    terms = {
        o: kept[n].astype(jnp.float32) + got[n].astype(jnp.float32)
        for n, o in enumerate(offsets[:low])
    }
    for bit in bits[:-1]:
        for o in sorted([o for o in terms if o & bit], reverse=True):
            term = swap(terms.pop(o).astype(jnp.bfloat16), "shard", shard_count, bit)
            terms[o ^ bit] = terms[o ^ bit] + term.astype(jnp.float32)
    done = terms[0].reshape(groups, row_count, features)
    other = swap(done[1].astype(jnp.bfloat16), "group", groups, 1).astype(jnp.float32)
    near = jnp.where(in_half, done[0], other)
    away = jnp.where(in_half, other, done[0]).astype(jnp.bfloat16)
    back = swap(away, "shard", shard_count, half_count).astype(jnp.float32)
    input_grad = (near + back).astype(jnp.bfloat16)

    w_updated, m_new, v_new, fresh = update_tiles(
        owned, row, piece, lane, x_parts, half_count, cot_turned,
        w_copy.reshape(w_master.shape), adam_m, adam_v,
    )
    tiles = fresh + swap(fresh, "group", groups, 1)
    rollout_tiles = tiles.reshape(col_tiles, CAP, TILE, TILE)

    partial, m_updated = finish_state(
        owned, row, adam_m, m_new, x_parts[: 2 * low], half_low
    )
    mine, give = turned_product(x_parts[2 * low :], half_high, partial, turn)
    (v_updated,) = finish_state(owned, row, adam_v, v_new)
    taken = swap(give, "group", groups, 1).astype(jnp.float32)
    projected = (mine + taken).astype(jnp.bfloat16)
    return (projected, input_grad, w_updated, m_updated, v_updated, rollout_tiles)


def any_shards(groups, shard_count, rollout_rows, assign, cotangent, w_master, adam_m, adam_v, tile_mask):
    group_at = lax.axis_index("group")
    shard_at = lax.axis_index("shard")
    row_count, features = rollout_rows.shape
    width = cotangent.shape[1]
    col_tiles = width // TILE
    row_tiles = w_master.shape[0] // TILE
    per_group = shard_count // groups
    row_total = groups * row_count
    order = jnp.arange(per_group, dtype=jnp.int32)
    w_copy, half = cast_pass(w_master.reshape(per_group, -1, width), order)
    x_cols = lax.all_gather(rollout_rows, "group", axis=0, tiled=True)
    x_full = lax.all_gather(x_cols, "shard", axis=0)
    x_all = lax.dynamic_slice_in_dim(x_full, group_at * per_group, per_group, 0)
    cot_all = lax.all_gather(cotangent, "group", axis=0, tiled=True)
    middle = row_total // 2
    products = back_product(cot_all[:middle], cot_all[middle:], half)
    products = products.reshape(per_group, groups, row_count, features)
    products = products.transpose(1, 0, 2, 3).reshape(shard_count * row_count, features)
    summed = lax.psum_scatter(products, "shard", scatter_dimension=0, tiled=True)
    moves = [
        (g * shard_count + r * per_group + k, r * shard_count + g * per_group + k)
        for g in range(groups)
        for r in range(groups)
        for k in range(per_group)
    ]
    input_grad = lax.ppermute(summed, ("group", "shard"), moves)
    pick = (jnp.arange(row_total)[:, None] == assign[None, :]).astype(jnp.bfloat16)
    cot_turned = jnp.dot(pick, cot_all, preferred_element_type=jnp.float32).astype(jnp.bfloat16)
    partial = jnp.take(forward_product(x_all, half), assign, axis=0)
    projected = lax.psum_scatter(partial, "group", scatter_dimension=0, tiled=True)
    projected = projected.astype(jnp.bfloat16)
    owned, row = owned_slots(tile_mask, group_at, shard_at, row_tiles, col_tiles)
    per_block = features // TILE
    piece = jnp.clip(row // per_block, 0, per_group - 1)
    lane = lax.rem(row + row_tiles * groups, per_block)
    w_updated, m_new, v_new, fresh = update_tiles(
        owned, row, piece, lane, list(x_all), per_group, cot_turned,
        w_copy.reshape(w_master.shape), adam_m, adam_v,
    )
    (m_updated,) = finish_state(owned, row, adam_m, m_new)
    (v_updated,) = finish_state(owned, row, adam_v, v_new)
    rollout_tiles = lax.psum(fresh, "group").reshape(col_tiles, CAP, TILE, TILE)
    return (projected, input_grad, w_updated, m_updated, v_updated, rollout_tiles)


def solution(mesh):
    groups, shard_count = mesh.shape["group"], mesh.shape["shard"]
    paired = groups == 2 and shard_count == 16
    inner = functools.partial(pair_shards if paired else any_shards, groups, shard_count)

    placed = (
        P("group", "shard"),
        P(),
        P("group", "shard"),
        P("group", "shard"),
        P("group", "shard"),
        P("group", "shard"),
        P(),
    )
    return jax.shard_map(
        inner,
        mesh=mesh,
        in_specs=placed,
        out_specs=(
            P("group", "shard"),
            P("group", "shard"),
            P("group", "shard"),
            P("group", "shard"),
            P("group", "shard"),
            P("shard", None, None, None),
        ),
        check_vma=False,
    )
```

```python
import functools

import jax
import jax.numpy as jnp
from jax import lax
from jax.experimental import pallas as pl
from jax.experimental.pallas import tpu as pltpu
from jax.sharding import PartitionSpec as P


TILE = 128
CAP = 6


beta_one = 0.9
beta_two = 0.999
learn_rate = 0.02
eps_adam = 1e-08
bias_one = 1.0 - 0.9**10
bias_two = 1.0 - 0.999**10


def stream_kernel(count, first, order, *refs):
    products = len(refs) > 10
    if products:
        near_ref, other_ref, w_ref, _, copy_ref, half_ref, out_ref, *rest = refs
        w_buf, half_buf, out_buf, load_sem, copy_sem, half_sem, out_sem = rest
        cot = jnp.concatenate([near_ref[...], other_ref[...]], axis=0)
    else:
        w_ref, copy_ref, half_ref, w_buf, half_buf, load_sem, copy_sem, half_sem = refs

    def load(n):
        return pltpu.make_async_copy(w_ref.at[order[first + n]], w_buf.at[n], load_sem.at[n])

    def stores(n):
        put = pltpu.make_async_copy
        some = [
            put(w_buf.at[n], copy_ref.at[order[first + n]], copy_sem.at[n]),
            put(half_buf.at[n], half_ref.at[n], half_sem.at[n]),
        ]
        return some + ([put(out_buf.at[n], out_ref.at[n], out_sem.at[n])] if products else [])

    for n in range(count):
        load(n).start()
    for n in range(count):
        load(n).wait()
        half = w_buf[n].astype(jnp.bfloat16)
        half_buf[n] = half
        copies = stores(n)
        copies[0].start()
        copies[1].start()
        if products:
            out_buf[n] = lax.dot_general(
                cot, half, (((1,), (1,)), ((), ())), preferred_element_type=jnp.float32
            ).astype(out_buf.dtype)
            copies[2].start()
    for n in range(count):
        for copy in stores(n):
            copy.wait()


def stream_pass(blocks, order, count, first=0, pair=(), copied=None, after=()):
    _, depth, width = blocks.shape
    smem = pl.BlockSpec(memory_space=pltpu.SMEM)
    vmem = pl.BlockSpec(memory_space=pltpu.VMEM)
    hbm = pl.BlockSpec(memory_space=pl.ANY)
    outs = [
        jax.ShapeDtypeStruct(blocks.shape, jnp.float32),
        jax.ShapeDtypeStruct((count, depth, width), jnp.bfloat16),
    ]
    scratch = [
        pltpu.VMEM((count, depth, width), jnp.float32),
        pltpu.VMEM((count, depth, width), jnp.bfloat16),
    ]
    more, rows = [], 0
    if pair:
        rows = pair[0].shape[0] + pair[1].shape[0]
        outs.append(jax.ShapeDtypeStruct((count, rows, depth), jnp.bfloat16))
        scratch.append(pltpu.VMEM((count, rows, depth), jnp.bfloat16))
        more = [copied]
    kept = len(pair) + 1 + len(more)
    body = functools.partial(stream_kernel, count, first)

    def kernel(order_ref, *refs):
        body(order_ref, *refs[:kept], *refs[kept + len(after) :])

    return pl.pallas_call(
        kernel,
        out_shape=outs,
        in_specs=[smem] + [vmem] * len(pair) + [hbm] * (1 + len(more) + len(after)),
        out_specs=[hbm] * len(outs),
        scratch_shapes=scratch + [pltpu.SemaphoreType.DMA((count,))] * (len(outs) + 1),
        input_output_aliases={1 + len(pair) + 1: 0} if more else {},
        cost_estimate=pl.CostEstimate(
            flops=2 * count * rows * width * depth,
            bytes_accessed=count * depth * (10 * width + 2 * rows),
            transcendentals=0,
        ),
        name="stream_pass",
    )(order, *pair, blocks, *more, *after)


def back_kernel(near_ref, other_ref, half_ref, out_ref, cot_ref):
    rows = near_ref.shape[0]

    @pl.when(pl.program_id(0) == 0)
    def _():
        cot_ref[:rows, :] = near_ref[...]
        cot_ref[rows:, :] = other_ref[...]

    out_ref[0] = lax.dot_general(
        cot_ref[...], half_ref[0], (((1,), (1,)), ((), ())), preferred_element_type=jnp.float32
    ).astype(out_ref.dtype)


def back_product(near, other, half):
    count, depth, width = half.shape
    rows = near.shape[0] + other.shape[0]
    vmem = pl.BlockSpec(memory_space=pltpu.VMEM)
    return pl.pallas_call(
        back_kernel,
        out_shape=jax.ShapeDtypeStruct((count, rows, depth), jnp.bfloat16),
        grid=(count,),
        in_specs=[vmem, vmem, pl.BlockSpec((1, depth, width), lambda i: (i, 0, 0))],
        out_specs=pl.BlockSpec((1, rows, depth), lambda i: (i, 0, 0)),
        scratch_shapes=[pltpu.VMEM((rows, width), jnp.bfloat16)],
        cost_estimate=pl.CostEstimate(
            flops=2 * count * rows * width * depth,
            bytes_accessed=2 * count * depth * (width + rows),
            transcendentals=0,
        ),
        name="back_product",
    )(near, other, half)


def turn_kernel(near_ref, other_ref, turn_ref, out_ref):
    rows = near_ref.shape[0]
    place = lax.broadcasted_iota(jnp.int32, (2 * rows, 2 * rows), 0)
    chosen = (place == turn_ref[...]).astype(jnp.bfloat16)
    cot = jnp.concatenate([near_ref[...], other_ref[...]], axis=0)
    out_ref[...] = jnp.dot(chosen, cot, preferred_element_type=jnp.float32).astype(jnp.bfloat16)


def turn_rows(near, other, turn):
    rows, width = near.shape
    vmem = pl.BlockSpec(memory_space=pltpu.VMEM)
    return pl.pallas_call(
        turn_kernel,
        out_shape=jax.ShapeDtypeStruct((2 * rows, width), jnp.bfloat16),
        in_specs=[vmem] * 3,
        out_specs=vmem,
        cost_estimate=pl.CostEstimate(
            flops=8 * rows * rows * width, bytes_accessed=8 * rows * width, transcendentals=0
        ),
        name="turn_rows",
    )(near, other, turn)


def forward_kernel(x_ref, w_ref, out_ref):
    product = jnp.dot(x_ref[0], w_ref[0], preferred_element_type=jnp.float32)

    @pl.when(pl.program_id(0) == 0)
    def _():
        out_ref[...] = product

    @pl.when(pl.program_id(0) > 0)
    def _():
        out_ref[...] += product


def forward_product(x, half):
    count, rows, depth = x.shape
    width = half.shape[2]
    return pl.pallas_call(
        forward_kernel,
        out_shape=jax.ShapeDtypeStruct((rows, width), jnp.float32),
        grid=(count,),
        in_specs=[
            pl.BlockSpec((1, rows, depth), lambda i: (i, 0, 0)),
            pl.BlockSpec((1, depth, width), lambda i: (i, 0, 0)),
        ],
        out_specs=pl.BlockSpec((rows, width), lambda i: (0, 0)),
        cost_estimate=pl.CostEstimate(
            flops=2 * count * rows * width * depth,
            bytes_accessed=2 * count * depth * (rows + width),
            transcendentals=0,
        ),
        name="forward_product",
    )(x, half)


def tile_kernel(slots, count, sides, owned, row, piece, lane, *refs):
    x_refs = refs[: count * sides]
    (
        cot_ref, w_in, m_in, v_in, w_out, m_out, v_out, fresh_ref,
        w_buf, m_buf, v_buf, x_buf, load_sem, store_sem,
    ) = refs[count * sides :]
    parts = ((w_in, w_buf), (m_in, m_buf), (v_in, v_buf))
    rows = x_refs[0].shape[0]

    def window(ref, i):
        return ref.at[
            pl.ds(pl.multiple_of(row[i] * TILE, TILE), TILE),
            pl.ds(pl.multiple_of(i // CAP * TILE, TILE), TILE),
        ]

    def load(i, k):
        source, buf = parts[k]
        return pltpu.make_async_copy(window(source, i), buf.at[i], load_sem.at[k, i])

    def store(i, k):
        target = (window(w_out, i), m_out.at[i], v_out.at[i])[k]
        return pltpu.make_async_copy(parts[k][1].at[i], target, store_sem.at[k, i])

    @pl.loop(0, slots)
    def _(i):
        @pl.when(owned[i] > 0)
        def _():
            for k in range(3):
                load(i, k).start()

    @pl.loop(0, slots)
    def _(i):
        @pl.when(owned[i] > 0)
        def _():
            columns = pl.ds(pl.multiple_of(lane[i] * TILE, TILE), TILE)
            for n in range(count):

                @pl.when(piece[i] == n)
                def _():
                    for side in range(sides):
                        x_buf[side * rows : (side + 1) * rows, :] = x_refs[n * sides + side][
                            :, columns
                        ]

            cot = cot_ref[:, pl.ds(pl.multiple_of(i // CAP * TILE, TILE), TILE)]
            gradient = lax.dot_general(
                x_buf[...], cot, (((0,), (0,)), ((), ())), preferred_element_type=jnp.float32
            )
            for k in range(3):
                load(i, k).wait()
            m = beta_one * m_buf[i] + (1.0 - beta_one) * gradient
            v = beta_two * v_buf[i] + (1.0 - beta_two) * gradient * gradient
            step = m / bias_one / (jnp.sqrt(v / bias_two) + eps_adam)
            w = w_buf[i] - learn_rate * step
            w_buf[i], m_buf[i], v_buf[i] = w, m, v
            fresh_ref[i] = w.astype(jnp.bfloat16)
            for k in range(3):
                store(i, k).start()

        @pl.when(owned[i] == 0)
        def _():
            fresh_ref[i] = jnp.zeros((TILE, TILE), jnp.bfloat16)

    @pl.loop(0, slots)
    def _(i):
        @pl.when(owned[i] > 0)
        def _():
            for k in range(3):
                store(i, k).wait()


def update_tiles(owned, row, piece, lane, x_parts, count, cot, w, m, v):
    slots = owned.shape[0]
    sides = len(x_parts) // count
    smem = pl.BlockSpec(memory_space=pltpu.SMEM)
    vmem = pl.BlockSpec(memory_space=pltpu.VMEM)
    hbm = pl.BlockSpec(memory_space=pl.ANY)
    state = jax.ShapeDtypeStruct((slots, TILE, TILE), jnp.float32)
    buf = pltpu.VMEM((slots, TILE, TILE), jnp.float32)
    sems = pltpu.SemaphoreType.DMA((3, slots))
    return pl.pallas_call(
        functools.partial(tile_kernel, slots, count, sides),
        out_shape=(
            jax.ShapeDtypeStruct(w.shape, w.dtype),
            state,
            state,
            jax.ShapeDtypeStruct(state.shape, jnp.bfloat16),
        ),
        in_specs=[smem] * 4 + [vmem] * (len(x_parts) + 1) + [hbm] * 3,
        out_specs=(hbm, hbm, hbm, vmem),
        scratch_shapes=[buf, buf, buf, pltpu.VMEM((cot.shape[0], TILE), jnp.bfloat16)]
        + [sems, sems],
        input_output_aliases={5 + len(x_parts): 0},
        cost_estimate=pl.CostEstimate(
            flops=2 * slots * TILE * TILE * cot.shape[0],
            bytes_accessed=26 * slots * TILE * TILE,
            transcendentals=slots * TILE * TILE,
        ),
        name="update_tiles",
    )(owned, row, piece, lane, *x_parts, cot, w, m, v)


CHUNKS = 8
DEPTH = 8


def finish_steps(slots, owned, row, a_ref, new_ref, out_ref, ring, tiles, sems, work):
    in_sem, out_sem, tile_sem = sems
    height = ring.shape[1]

    def load(c):
        source = a_ref.at[pl.ds(c * height, height), :]
        return pltpu.make_async_copy(source, ring.at[c % DEPTH], in_sem.at[c % DEPTH])

    def store(c):
        target = out_ref.at[pl.ds(c * height, height), :]
        return pltpu.make_async_copy(ring.at[c % DEPTH], target, out_sem.at[c % DEPTH])

    def fetch(i):
        return pltpu.make_async_copy(new_ref.at[i], tiles.at[i], tile_sem.at[i])

    def put(i):
        target = out_ref.at[
            pl.ds(pl.multiple_of(row[i] * TILE, TILE), TILE),
            pl.ds(pl.multiple_of(i // CAP * TILE, TILE), TILE),
        ]
        return pltpu.make_async_copy(tiles.at[i], target, tile_sem.at[i])

    def each(do):
        @pl.loop(0, slots)
        def _(i):
            @pl.when(owned[i] > 0)
            def _():
                do(i)

    for c in range(min(DEPTH, CHUNKS)):
        load(c).start()
    each(lambda i: fetch(i).start())
    waited = 0
    for c in range(CHUNKS):
        if c >= 2 and c - 2 + DEPTH < CHUNKS:
            store(c - 2).wait()
            waited = c - 1
            load(c - 2 + DEPTH).start()
        load(c).wait()
        store(c).start()
        if c < len(work):
            work[c]()
    each(lambda i: fetch(i).wait())
    for c in range(waited, CHUNKS):
        store(c).wait()
    each(lambda i: put(i).start())
    for step in work[CHUNKS:]:
        step()
    each(lambda i: put(i).wait())


def product_steps(count, x_refs, w_ref, base_ref, sum_ref):
    rows = x_refs[0].shape[0]

    def step(k):
        n, side = divmod(k, 2)
        into = pl.ds(side * rows, rows)
        product = jnp.dot(x_refs[k][...], w_ref[n], preferred_element_type=jnp.float32)
        if n > 0:
            sum_ref[into, :] += product
        elif base_ref is not None:
            sum_ref[into, :] = base_ref[into, :] + product
        else:
            sum_ref[into, :] = product

    return [functools.partial(step, k) for k in range(2 * count)]


def low_kernel(slots, count, owned, row, *refs):
    w_ref, a_ref, new_ref, sum_ref, out_ref, ring, tiles, *sems = refs[2 * count :]
    work = product_steps(count, refs[: 2 * count], w_ref, None, sum_ref)
    finish_steps(slots, owned, row, a_ref, new_ref, out_ref, ring, tiles, sems, work)


def turned_kernel(count, *refs):
    w_ref, base_ref, turn_ref, mine_ref, give_ref, sum_ref = refs[2 * count :]
    for step in product_steps(count, refs[: 2 * count], w_ref, base_ref, sum_ref):
        step()
    total, rows = sum_ref.shape[0], mine_ref.shape[0]
    place = lax.broadcasted_iota(jnp.int32, (total, rows), 0)

    def rows_of(side, values):
        chosen = place == turn_ref[:, side * rows : (side + 1) * rows]
        return lax.dot_general(
            chosen.astype(jnp.bfloat16), values, (((0,), (0,)), ((), ())),
            preferred_element_type=jnp.float32,
        )

    value = sum_ref[...]
    head = value.astype(jnp.bfloat16)
    rest = (value - head.astype(jnp.float32)).astype(jnp.bfloat16)
    give_ref[...] = rows_of(1, head).astype(jnp.bfloat16)
    mine_ref[...] = rows_of(0, head) + rows_of(0, rest)


def turned_product(parts, half, base, turn):
    count = half.shape[0]
    rows, depth = parts[0].shape
    width = half.shape[2]
    vmem = pl.BlockSpec(memory_space=pltpu.VMEM)
    return pl.pallas_call(
        functools.partial(turned_kernel, count),
        out_shape=(
            jax.ShapeDtypeStruct((rows, width), jnp.float32),
            jax.ShapeDtypeStruct((rows, width), jnp.bfloat16),
        ),
        in_specs=[vmem] * (2 * count + 3),
        out_specs=(vmem, vmem),
        scratch_shapes=[pltpu.VMEM((2 * rows, width), jnp.float32)],
        cost_estimate=pl.CostEstimate(
            flops=4 * count * rows * width * depth,
            bytes_accessed=2 * count * depth * (2 * rows + width),
            transcendentals=0,
        ),
        name="turned_product",
    )(*parts, half, base, turn)


def plain_kernel(slots, owned, row, a_ref, new_ref, out_ref, ring, tiles, *sems):
    finish_steps(slots, owned, row, a_ref, new_ref, out_ref, ring, tiles, sems, [])


def finish_state(owned, row, a, new, parts=(), half=None):
    slots = owned.shape[0]
    count = len(parts) // 2
    smem = pl.BlockSpec(memory_space=pltpu.SMEM)
    vmem = pl.BlockSpec(memory_space=pltpu.VMEM)
    hbm = pl.BlockSpec(memory_space=pl.ANY)
    outs, operands, scratch = [], list(parts), []
    kernel = functools.partial(plain_kernel, slots)
    if parts:
        operands.append(half)
        kernel = functools.partial(low_kernel, slots, count)
        outs = [jax.ShapeDtypeStruct((2 * parts[0].shape[0], half.shape[2]), jnp.float32)]
    scratch += [
        pltpu.VMEM((DEPTH, a.shape[0] // CHUNKS, a.shape[1]), a.dtype),
        pltpu.VMEM((slots, TILE, TILE), a.dtype),
        pltpu.SemaphoreType.DMA((DEPTH,)),
        pltpu.SemaphoreType.DMA((DEPTH,)),
        pltpu.SemaphoreType.DMA((slots,)),
    ]
    flops = sum(2 * p.size * half.shape[2] for p in parts)
    return pl.pallas_call(
        kernel,
        out_shape=outs + [jax.ShapeDtypeStruct(a.shape, a.dtype)],
        in_specs=[smem, smem] + [vmem] * len(operands) + [hbm, hbm],
        out_specs=[vmem] * len(outs) + [hbm],
        scratch_shapes=scratch,
        cost_estimate=pl.CostEstimate(
            flops=flops, bytes_accessed=8 * a.size, transcendentals=0
        ),
        name="finish_state",
    )(owned, row, *operands, a, new)


def swap(a, axis, size, bit):
    return lax.ppermute(a, axis, [(i, i ^ bit) for i in range(size)])


def owned_slots(tile_mask, group_at, shard_at, row_tiles, col_tiles):
    mask_cols = lax.dynamic_slice_in_dim(tile_mask, shard_at * col_tiles, col_tiles, 1)
    count = tile_mask.shape[0]
    at = jnp.arange(count)
    before = (at[None, :] < at[:, None]).astype(jnp.float32)
    rank = jnp.dot(before, mask_cols.astype(jnp.float32)).astype(jnp.int32)
    hit = (mask_cols[:, :, None] > 0) & (rank[:, :, None] == jnp.arange(CAP)[None, None, :])
    row = jnp.sum(jnp.where(hit, at[:, None, None], 0), axis=0).reshape(-1)
    live = jnp.sum(hit.astype(jnp.int32), axis=0).reshape(-1)
    owned = jnp.where(row // row_tiles == group_at, live, 0)
    return owned, row - group_at * row_tiles


def pair_shards(groups, shard_count, rollout_rows, assign, cotangent, w_master, adam_m, adam_v, tile_mask):
    group_at = lax.axis_index("group")
    shard_at = lax.axis_index("shard")
    row_count, features = rollout_rows.shape
    width = cotangent.shape[1]
    col_tiles = width // TILE
    row_tiles = w_master.shape[0] // TILE
    half_count = shard_count // 2
    bits = [half_count >> (k + 1) for k in range(half_count.bit_length() - 1)]
    offsets = [0]
    for bit in bits:
        offsets = offsets + [o | bit for o in offsets]
    base = shard_at % half_count
    order = base ^ jnp.asarray(offsets, jnp.int32)
    in_half = shard_at // half_count == group_at

    blocks = w_master.reshape(half_count, features, width)
    low = half_count // 2

    row_total = groups * row_count
    start = group_at * row_count
    turned = jnp.where(group_at == 0, assign, jnp.concatenate([assign[row_count:], assign[:row_count]]))
    turned = jnp.where(turned >= start, turned - start, turned + row_total - start)

    owned, row = owned_slots(tile_mask, group_at, shard_at, row_tiles, col_tiles)
    per_block = features // TILE
    block = jnp.clip(row // per_block, 0, half_count - 1) ^ base
    piece = sum(jnp.where(block & bit > 0, 1 << k, 0) for k, bit in enumerate(bits))
    lane = lax.rem(row + row_tiles * groups, per_block)
    piece = piece.astype(jnp.int32)
    turn = turned.reshape(1, row_total)

    cot_other = swap(cotangent, "group", groups, 1)
    far = swap(rollout_rows, "shard", shard_count, half_count)
    w_copy, half_high = stream_pass(blocks, order, low, low, after=(owned, row, piece, lane, turn))
    sent = back_product(cotangent, cot_other, half_high)
    got = swap(sent, "shard", shard_count, bits[-1])
    keep = jnp.where(in_half, rollout_rows, far)
    give = jnp.where(in_half, far, rollout_rows)
    x_parts = [keep, swap(give, "group", groups, 1)]
    for bit in bits:
        held = list(x_parts)
        for part in held:
            x_parts.append(swap(part, "shard", shard_count, bit))

    w_copy, half_low, kept = stream_pass(
        blocks, order, low, 0, (cotangent, cot_other), w_copy
    )
    cot_turned = turn_rows(cotangent, cot_other, turn)
    terms = {
        o: kept[n].astype(jnp.float32) + got[n].astype(jnp.float32)
        for n, o in enumerate(offsets[:low])
    }
    for bit in bits[:-1]:
        for o in sorted([o for o in terms if o & bit], reverse=True):
            term = swap(terms.pop(o).astype(jnp.bfloat16), "shard", shard_count, bit)
            terms[o ^ bit] = terms[o ^ bit] + term.astype(jnp.float32)
    done = terms[0].reshape(groups, row_count, features)
    other = swap(done[1].astype(jnp.bfloat16), "group", groups, 1).astype(jnp.float32)
    near = jnp.where(in_half, done[0], other)
    away = jnp.where(in_half, other, done[0]).astype(jnp.bfloat16)
    back = swap(away, "shard", shard_count, half_count).astype(jnp.float32)
    input_grad = (near + back).astype(jnp.bfloat16)

    w_updated, m_new, v_new, fresh = update_tiles(
        owned, row, piece, lane, x_parts, half_count, cot_turned,
        w_copy.reshape(w_master.shape), adam_m, adam_v,
    )
    tiles = fresh + swap(fresh, "group", groups, 1)
    rollout_tiles = tiles.reshape(col_tiles, CAP, TILE, TILE)

    partial, m_updated = finish_state(
        owned, row, adam_m, m_new, x_parts[: 2 * low], half_low
    )
    mine, give = turned_product(x_parts[2 * low :], half_high, partial, turn)
    (v_updated,) = finish_state(owned, row, adam_v, v_new)
    taken = swap(give, "group", groups, 1).astype(jnp.float32)
    projected = (mine + taken).astype(jnp.bfloat16)
    return (projected, input_grad, w_updated, m_updated, v_updated, rollout_tiles)


def any_shards(groups, shard_count, rollout_rows, assign, cotangent, w_master, adam_m, adam_v, tile_mask):
    group_at = lax.axis_index("group")
    shard_at = lax.axis_index("shard")
    row_count, features = rollout_rows.shape
    width = cotangent.shape[1]
    col_tiles = width // TILE
    row_tiles = w_master.shape[0] // TILE
    per_group = shard_count // groups
    row_total = groups * row_count
    order = jnp.arange(per_group, dtype=jnp.int32)
    w_copy, half = stream_pass(w_master.reshape(per_group, -1, width), order, per_group)
    x_cols = lax.all_gather(rollout_rows, "group", axis=0, tiled=True)
    x_full = lax.all_gather(x_cols, "shard", axis=0)
    x_all = lax.dynamic_slice_in_dim(x_full, group_at * per_group, per_group, 0)
    cot_all = lax.all_gather(cotangent, "group", axis=0, tiled=True)
    middle = row_total // 2
    products = back_product(cot_all[:middle], cot_all[middle:], half)
    products = products.reshape(per_group, groups, row_count, features)
    products = products.transpose(1, 0, 2, 3).reshape(shard_count * row_count, features)
    summed = lax.psum_scatter(products, "shard", scatter_dimension=0, tiled=True)
    moves = [
        (g * shard_count + r * per_group + k, r * shard_count + g * per_group + k)
        for g in range(groups)
        for r in range(groups)
        for k in range(per_group)
    ]
    input_grad = lax.ppermute(summed, ("group", "shard"), moves)
    pick = (jnp.arange(row_total)[:, None] == assign[None, :]).astype(jnp.bfloat16)
    cot_turned = jnp.dot(pick, cot_all, preferred_element_type=jnp.float32).astype(jnp.bfloat16)
    partial = jnp.take(forward_product(x_all, half), assign, axis=0)
    projected = lax.psum_scatter(partial, "group", scatter_dimension=0, tiled=True)
    projected = projected.astype(jnp.bfloat16)
    owned, row = owned_slots(tile_mask, group_at, shard_at, row_tiles, col_tiles)
    per_block = features // TILE
    piece = jnp.clip(row // per_block, 0, per_group - 1)
    lane = lax.rem(row + row_tiles * groups, per_block)
    w_updated, m_new, v_new, fresh = update_tiles(
        owned, row, piece, lane, list(x_all), per_group, cot_turned,
        w_copy.reshape(w_master.shape), adam_m, adam_v,
    )
    (m_updated,) = finish_state(owned, row, adam_m, m_new)
    (v_updated,) = finish_state(owned, row, adam_v, v_new)
    rollout_tiles = lax.psum(fresh, "group").reshape(col_tiles, CAP, TILE, TILE)
    return (projected, input_grad, w_updated, m_updated, v_updated, rollout_tiles)


def solution(mesh):
    groups, shard_count = mesh.shape["group"], mesh.shape["shard"]
    paired = groups == 2 and shard_count == 16
    inner = functools.partial(pair_shards if paired else any_shards, groups, shard_count)

    placed = (
        P("group", "shard"),
        P(),
        P("group", "shard"),
        P("group", "shard"),
        P("group", "shard"),
        P("group", "shard"),
        P(),
    )
    return jax.shard_map(
        inner,
        mesh=mesh,
        in_specs=placed,
        out_specs=(
            P("group", "shard"),
            P("group", "shard"),
            P("group", "shard"),
            P("group", "shard"),
            P("group", "shard"),
            P("shard", None, None, None),
        ),
        check_vma=False,
    )
```
